32 devices in a mesh: dp: 16 (over z, y, x), blk: 2 (over core).
Axes of the slice: x: 2, y: 2, z: 4, core: 2. Of those that a mesh axis runs over, the one named last changes fastest.
Arguments:
- vectors: float32 [16384, 96], P('dp'), may hold values from -16 to 16
- codes: int32 [16384, 8], P('dp'), may hold values from 0 to 255, as said below
- weights: bfloat16 [16384], P('dp'), may hold values from 0.25 to 4
- ridge: float32 [1], replicated, may hold values from 0.1 to 0.5
Outputs:
- codebooks: float32 [8, 256, 96], replicated
- residual: float32 [16384, 96], P('dp')
- distortion: float32 [], replicated
The draws below stay inside these ranges and needn't reach their ends.
Inputs may be any that keep to these rules, and one draw needn't show every extreme that they name: `codes`: 8 codebook indices per vector.
All inputs are finite; a program needn't handle non-finite values.
Results may differ from the reference program's by a relative error of at most 0.0003.
Values sent between devices are 32-bit elements; how exact they have to be, the bound alone decides.
A program may use at most 128 MiB of HBM per device.

```python
import math
import jax
import jax.numpy as jnp
from jax import lax

D = 96
K = 256
M = 8
ITERS = 8
ROWS = 16384


def shared_codes(key):
    base = jax.random.fold_in(key, 11)
    keys = jax.random.split(base, 4)
    perms = jax.vmap(lambda single: jax.random.permutation(single, K))(jax.random.split(keys[0], M))
    perms = perms.astype(jnp.int32)
    first = jax.random.randint(keys[1], (ROWS, M), 0, K).astype(jnp.int32)
    second = jax.random.randint(keys[2], (ROWS, M), 0, K).astype(jnp.int32)
    ranks = jnp.minimum(first, second)
    tied = jax.random.randint(keys[3], (ROWS, 1), 0, 2).astype(jnp.int32)
    ranks = jnp.where(tied == 1, ranks[:, :1], ranks).astype(jnp.int32)
    return perms[jnp.arange(M)[None, :], ranks].astype(jnp.int32)


def draw_codes(key, part):
    return shared_codes(key)


def draw_vectors(key, part):
    codes = shared_codes(key)
    keys = jax.random.split(jax.random.fold_in(key, 23), 2)
    truth = 0.5 * jax.random.truncated_normal(keys[0], -3.0, 3.0, (M, K, D), jnp.float32)
    recon = jnp.zeros((ROWS, D), jnp.float32)
    for book in range(M):
        recon = recon + jnp.take(truth[book], codes[:, book], axis=0)
    position = jnp.arange(ROWS, dtype=jnp.float32) / ROWS
    level = (0.3 * (1.0 + 2.0 * position))[:, None]
    noise = jax.random.truncated_normal(keys[1], -4.0, 4.0, (ROWS, D), jnp.float32)
    return recon + level * noise


def steps_of(own_key, dims, cuts, least, high):
    factor_of = 1.0
    for dim, shards_of in cuts:
        steps = jax.random.uniform(jax.random.fold_in(jax.random.fold_in(own_key, 6), dim), (shards_of,), jnp.float32, least / len(cuts), high / len(cuts))
        factor_of = factor_of * jnp.repeat(jnp.exp(steps), dims[dim] // shards_of).reshape((-1,) + (1,) * (len(dims) - 1 - dim))
    return factor_of


def setup_inputs(seed: int = 0) -> dict:
    arg_keys = jax.random.split(jax.random.key(seed), 5)
    vectors = draw_vectors(jax.random.fold_in(arg_keys[4], 71), 0)
    codes = draw_codes(jax.random.fold_in(arg_keys[4], 71), 0)
    weights = jnp.clip(jnp.exp(math.log(4.0) - 2.7725887 * jax.random.uniform(arg_keys[2], (ROWS,), jnp.float32) ** steps_of(arg_keys[2], (ROWS,), ((0, 16),), -0.2, 0.2)), 0.25, 4.0).astype(jnp.bfloat16)
    ridge = jnp.clip(jnp.exp(jax.random.uniform(arg_keys[3], (1,), jnp.float32, math.log(0.1), math.log(0.5))), 0.1, 0.5)
    return {"vectors": vectors, "codes": codes, "weights": weights, "ridge": ridge}


HIGH = lax.Precision.HIGHEST


def reference(vectors, codes, weights, ridge):
    rows = vectors.shape[0]
    mass = weights.astype(jnp.float32)
    weighted = vectors * mass[:, None]
    count_list = []
    sum_list = []
    for book in range(M):
        count_list.append(jax.ops.segment_sum(mass, codes[:, book], num_segments=K))
        sum_list.append(jax.ops.segment_sum(weighted, codes[:, book], num_segments=K))
    counts = jnp.stack(count_list)
    right = jnp.stack(sum_list).reshape(M * K, D)
    blocks = []
    for first in range(M):
        row_blocks = []
        for second in range(M):
            if first == second:
                row_blocks.append(jnp.diag(counts[first]))
            else:
                joint = codes[:, first] * K + codes[:, second]
                row_blocks.append(jax.ops.segment_sum(mass, joint, num_segments=K * K).reshape(K, K))
        blocks.append(jnp.concatenate(row_blocks, axis=1))
    gram = jnp.concatenate(blocks, axis=0)
    total_mass = jnp.sum(counts[0])
    lam = ridge[0] * total_mass / K
    precond = (counts + lam).reshape(M * K, 1)
    solution = jnp.zeros((M * K, D), jnp.float32)
    remain = right
    scaled = remain / precond
    direction = scaled
    inner = jnp.sum(remain * scaled, axis=0)
    for step in range(ITERS):
        image = jnp.dot(gram, direction, precision=HIGH) + lam * direction
        alpha = inner / jnp.sum(direction * image, axis=0)
        solution = solution + alpha * direction
        remain = remain - alpha * image
        scaled = remain / precond
        fresh = jnp.sum(remain * scaled, axis=0)
        direction = scaled + (fresh / inner) * direction
        inner = fresh
    codebooks = solution.reshape(M, K, D)
    recon = jnp.zeros_like(vectors)
    for book in range(M):
        recon = recon + jnp.take(codebooks[book], codes[:, book], axis=0)
    residual = vectors - recon
    distortion = jnp.sum(mass[:, None] * residual * residual) / (total_mass * D)
    return codebooks, residual, distortion
```

```python
import functools

import jax
import jax.numpy as jnp
from jax import lax
from jax.experimental import pallas as pl
from jax.experimental.pallas import tpu as pltpu
from jax.sharding import PartitionSpec as P

K = 256
M = 8
ITERS = 8
MESH = pl.DeviceIdType.MESH
HIGH = lax.Precision.HIGHEST
F32 = jnp.float32
BF16 = jnp.bfloat16
NT = (((1,), (1,)), ((), ()))


def vmem():
    return pl.BlockSpec(memory_space=pltpu.VMEM)


def split2(value):
    high = value.astype(BF16)
    low = (value - high.astype(F32)).astype(BF16)
    return high, low


def split3(value):
    high = value.astype(BF16)
    rest = value - high.astype(F32)
    middle = rest.astype(BF16)
    low = (rest - middle.astype(F32)).astype(BF16)
    return high, middle, low


def column_groups(groups, width):
    best = 1
    for count in range(1, groups + 1):
        if groups % count == 0 and width % count == 0 and (width // count) % 8 == 0:
            best = count
    return best


def hot_t(row, levels):
    return jnp.where(levels == row, jnp.ones((), BF16), jnp.zeros((), BF16))


def flip(value, mask, size):
    total, digit = 0, 1
    while digit < size:
        total = total + digit * lax.rem(value // digit + mask // digit % 2, 2)
        digit *= 2
    return total


def column(pieces):
    total = pieces[0]
    for piece in pieces[1:]:
        total = total + piece
    return jnp.sum(total, axis=1, keepdims=True)


def kernel(n, nblk, ncg, ridge_ref, codes_ref, mass_ref, vectors_ref, book_out, residual_out, sum_out,
           codes_all, mass_all, part, pieces, gram, halves, swap, solution, remain, direction, inverse,
           books, parts, gathered, send_sem, recv_sem, swap_send, swap_recv, far_send, far_recv,
           near_send, near_recv, sum_send, sum_recv):
    width, rows = vectors_ref.shape
    gsz = M // nblk
    cols = width // ncg
    me = lax.axis_index("dp")
    blk = lax.axis_index("blk")
    group, member = me // gsz, lax.rem(me, gsz)
    book = nblk * member + blk
    mine = lax.rem(group, ncg)
    bases = group - mine
    half = M // nblk
    peers = [(dm, db) for dm in range(gsz - 1, -1, -1) for db in range(nblk - 1, -1, -1) if (dm, db) != (0, 0)]

    def chip(k):
        return {"dp": lax.rem(me + k, n)}

    def team(dm, db):
        return {"dp": group * gsz + flip(member, dm, gsz), "blk": lax.rem(blk + db, nblk)}

    def far(k):
        return {"dp": (bases + lax.rem(mine + k, ncg)) * gsz + member, "blk": blk}

    def remote(source, target, send, recv, to):
        return pltpu.make_async_remote_copy(
            src_ref=source, dst_ref=target, send_sem=send, recv_sem=recv, device_id=to, device_id_type=MESH
        )

    def loop(function):
        def step(k, carry):
            function(k)
            return carry

        lax.fori_loop(1, n, step, 0)

    barrier = pltpu.get_barrier_semaphore()
    loop(lambda k: pl.semaphore_signal(barrier, inc=1, device_id=chip(k), device_id_type=MESH))
    others = [(dm, db) for dm, db in peers if db]
    for dm, db in others:
        pl.semaphore_signal(barrier, inc=1, device_id=team(dm, db), device_id_type=MESH)

    triple = jnp.concatenate(split3(vectors_ref[...]), axis=0)
    levels = lax.broadcasted_iota(jnp.int32, (K, rows), 0).astype(F32).astype(BF16)

    def spread(row, mass):
        return jnp.where(levels == row.astype(F32).astype(BF16), jnp.broadcast_to(mass, (K, rows)), jnp.zeros((), BF16))

    for m in range(gsz):
        hot = spread(codes_ref[pl.ds(nblk * m + blk, 1), :], mass_ref[...].astype(BF16))
        sums = lax.dot_general(triple, hot, NT, preferred_element_type=F32)
        total = sums[:width] + sums[width : 2 * width] + sums[2 * width :]
        for c in range(ncg):
            part[c, m] = total[c * cols : (c + 1) * cols]
    pl.semaphore_wait(barrier, n - 1 + len(others))

    def codes_copy(k):
        return remote(codes_ref, codes_all.at[me], send_sem.at[0, k], recv_sem.at[0, k], chip(k))

    def mass_copy(k):
        return remote(mass_ref, mass_all.at[me], send_sem.at[1, k], recv_sem.at[1, k], chip(k))

    def piece_copy(k):
        to = lax.rem(me + k, n)
        piece = part.at[lax.rem(to // gsz, ncg), lax.rem(to, gsz)]
        return remote(piece, pieces.at[me], send_sem.at[2, k], recv_sem.at[2, k], chip(k))

    def send_codes(k):
        codes_copy(k).start()
        mass_copy(k).start()

    loop(send_codes)

    codes_all[me] = codes_ref[...]
    mass_all[me] = mass_ref[...]
    pieces[me] = part[mine, member]
    gram[...] = jnp.zeros_like(gram)

    def block(q):
        return pl.ds(pl.multiple_of(q * K, K), K)

    def accumulate(source):
        weighted = spread(codes_all[source, pl.ds(book, 1), :], mass_all[source].astype(BF16))
        for j in range(1, M):
            other = lax.rem(book + j, M)
            hot = spread(codes_all[source, pl.ds(other, 1), :], jnp.ones((1, 1), BF16))
            gram[block(other), :] += lax.dot_general(hot, weighted, NT, preferred_element_type=F32)

    accumulate(me)

    def arrive(k):
        codes_copy(k).wait_recv()
        mass_copy(k).wait_recv()
        piece_copy(k).start()
        accumulate(lax.rem(me - k + n, n))

    loop(arrive)

    square = (K, K)
    own = jnp.sum(gram[block(lax.rem(book + 1, M)), :], axis=0, keepdims=True)
    diagonal = lax.broadcasted_iota(jnp.int32, square, 0) == lax.broadcasted_iota(jnp.int32, square, 1)
    gram[block(book), :] = jnp.where(diagonal, jnp.broadcast_to(own, square), 0.0)
    ones = jnp.ones((8, K), F32)
    for q in range(M):
        value = gram[block(q), :]
        high, low = split2(value)
        halves[block(q), :K] = high
        halves[block(q), K:] = low
        inverse[q] = lax.dot_general(ones, value, NT, precision=HIGH, preferred_element_type=F32)
    whole = jnp.sum(inverse[0, 0:1, :])
    lam = ridge_ref[0] * (whole / K)
    for q in range(M):
        inverse[q] = 1.0 / (inverse[q] + lam)

    loop(lambda k: piece_copy(k).wait_recv())
    right = lax.fori_loop(1, n, lambda s, total: total + pieces[s], pieces[0])

    streams = [(i, pl.ds(first, last - first), last - first) for i, (first, last) in enumerate([(c, c + 8) for c in range(0, cols, 8)])]

    def copies(stream, slot):
        i, span, _ = stream
        here = swap.at[slot, book, span]
        return [
            remote(here, here, swap_send.at[slot, i, j], swap_recv.at[slot, i, j], team(dm, db))
            for j, (dm, db) in enumerate(peers)
        ]

    def send(stream, slot, value):
        swap[slot, book, stream[1]] = value
        for copy in copies(stream, slot):
            copy.start()

    def receive(stream, slot):
        for copy in copies(stream, slot):
            copy.wait()

    def apply(stream):
        _, span, size = stream
        product = None
        for q in range(M):
            left = jnp.concatenate(split2(direction[q, span]), axis=0)
            term = jnp.dot(left, halves[pl.ds(q * K, K), :], preferred_element_type=F32)
            product = term if product is None else product + term
        return (product[:size, :K] + product[size:, :K]) + (product[:size, K:] + product[size:, K:])

    def begin(stream):
        _, span, _ = stream
        receive(stream, 0)
        terms = []
        for q in range(M):
            r = swap[0, q, span]
            z = r * inverse[q, 0:1, :]
            remain[q, span] = r
            direction[q, span] = z
            solution[q, span] = jnp.zeros_like(r)
            terms.append(r * z)
        send(stream, 1, apply(stream))
        return column(terms)

    def advance(stream, slot, inner):
        _, span, _ = stream
        receive(stream, slot)
        terms = []
        for q in range(M):
            d = direction[q, span]
            terms.append(d * (swap[slot, q, span] + lam * d))
        alpha = inner / column(terms)
        terms = []
        for q in range(M):
            d = direction[q, span]
            r = remain[q, span] - alpha * (swap[slot, q, span] + lam * d)
            solution[q, span] = solution[q, span] + alpha * d
            remain[q, span] = r
            terms.append(r * (r * inverse[q, 0:1, :]))
        fresh = column(terms)
        beta = fresh / inner
        for q in range(M):
            direction[q, span] = remain[q, span] * inverse[q, 0:1, :] + beta * direction[q, span]
        return fresh

    def iterate(step, inners):
        slot = lax.rem(step, 2)
        results = []
        for stream, inner in zip(streams, inners):
            results.append(advance(stream, slot, inner))
            send(stream, 1 - slot, apply(stream))
        return tuple(results)

    for stream in streams:
        first = stream[1].start
        send(stream, 0, right[first : first + stream[2]])
    inners = lax.fori_loop(1, ITERS, iterate, tuple(begin(stream) for stream in streams))
    for stream, inner in zip(streams, inners):
        advance(stream, ITERS % 2, inner)

    span = pl.ds(blk * half, half)
    away = [
        remote(solution.at[span], books.at[mine, span], far_send.at[k], far_recv.at[k], far(k)) for k in range(1, ncg)
    ]
    for copy in away:
        copy.start()
    for q in range(M):
        books[mine, q] = solution[q]
    relays = []
    for k in range(1, ncg):
        away[k - 1].wait_recv()
        there = books.at[lax.rem(mine - k + ncg, ncg), span]
        for db in range(1, nblk):
            relay = remote(there, there, near_send.at[k, db], near_recv.at[k, db], team(0, db))
            relay.start()
            relays.append(relay)
    for relay in relays:
        relay.wait()

    for q in range(M):
        value = jnp.concatenate([books[c, q] for c in range(ncg)], axis=0)
        book_out[q] = value
        high, low = split2(value)
        parts[q, :width, :] = high
        parts[q, width:, :] = low

    size = min(256, rows)
    short = lax.broadcasted_iota(jnp.int32, (K, size), 0).astype(F32).astype(BF16)

    def rebuild(turn, total):
        at = pl.ds(pl.multiple_of(turn * size, size), size)
        value = jnp.zeros((2 * width, size), F32)
        for q in range(M):
            row = codes_ref[q : q + 1, at].astype(F32).astype(BF16)
            value = value + jnp.dot(parts[q], hot_t(row, short), preferred_element_type=F32)
        residual = vectors_ref[:, at] - (value[:width] + value[width:])
        residual_out[:, at] = residual
        return total + mass_ref[:, at] * (residual * residual)

    total = lax.fori_loop(0, rows // size, rebuild, jnp.zeros((width, size), F32))
    gathered[me] = jnp.broadcast_to(jnp.sum(total, keepdims=True), (8, 128))

    def sum_copy(k):
        return remote(gathered.at[me], gathered.at[me], sum_send.at[k], sum_recv.at[k], chip(k))

    loop(lambda k: sum_copy(k).start())
    for copy in away:
        copy.wait_send()

    def drain(k):
        codes_copy(k).wait_send()
        mass_copy(k).wait_send()
        piece_copy(k).wait_send()

    loop(drain)
    loop(lambda k: sum_copy(k).wait())
    final = lax.fori_loop(1, n, lambda s, value: value + gathered[s], gathered[0])
    sum_out[...] = final / (whole * width)


def body(vectors, codes, weights, ridge):
    rows, width = vectors.shape
    n, nblk = lax.axis_size("dp"), lax.axis_size("blk")
    gsz = M // nblk
    ncg = column_groups(n // gsz, width)
    cols = width // ncg
    shape = jax.ShapeDtypeStruct
    dma = pltpu.SemaphoreType.DMA
    state = pltpu.VMEM((M, cols, K), F32)
    books, residual, distortion = pl.pallas_call(
        functools.partial(kernel, n, nblk, ncg),
        out_shape=(shape((M, width, K), F32), shape((width, rows), F32), shape((8, 128), F32)),
        in_specs=[pl.BlockSpec(memory_space=pltpu.SMEM)] + [vmem()] * 3,
        out_specs=(vmem(),) * 3,
        scratch_shapes=[
            pltpu.VMEM((n, M, rows), jnp.int32),
            pltpu.VMEM((n, 1, rows), F32),
            pltpu.VMEM((ncg, gsz, cols, K), F32),
            pltpu.VMEM((n, cols, K), F32),
            pltpu.VMEM((M * K, K), F32),
            pltpu.VMEM((M * K, 2 * K), BF16),
            pltpu.VMEM((2, M, cols, K), F32),
            state,
            state,
            state,
            pltpu.VMEM((M, 8, K), F32),
            pltpu.VMEM((ncg, M, cols, K), F32),
            pltpu.VMEM((M, 2 * width, K), BF16),
            pltpu.VMEM((n, 8, 128), F32),
            dma((3, n)),
            dma((3, n)),
            dma((2, 3, M)),
            dma((2, 3, M)),
            dma((ncg,)),
            dma((ncg,)),
            dma((ncg, nblk)),
            dma((ncg, nblk)),
            dma((n,)),
            dma((n,)),
        ],
        compiler_params=pltpu.CompilerParams(collective_id=0, has_side_effects=True),
        name="update",
    )(ridge, codes.T, weights.astype(F32)[None, :], vectors.T)
    return (books.transpose(0, 2, 1), residual.T, distortion[0, 0])


def solution(mesh):
    return jax.shard_map(
        body,
        mesh=mesh,
        in_specs=(P("dp", None), P("dp", None), P("dp"), P()),
        out_specs=(P(), P("dp", None), P()),
        check_vma=False,
    )
```

```python
import functools

import jax
import jax.numpy as jnp
from jax import lax
from jax.experimental import pallas as pl
from jax.experimental.pallas import tpu as pltpu
from jax.sharding import PartitionSpec as P

K = 256
M = 8
ITERS = 8
MESH = pl.DeviceIdType.MESH
HIGH = lax.Precision.HIGHEST
F32 = jnp.float32
BF16 = jnp.bfloat16
NT = (((1,), (1,)), ((), ()))


def vmem():
    return pl.BlockSpec(memory_space=pltpu.VMEM)


def split2(value):
    high = value.astype(BF16)
    low = (value - high.astype(F32)).astype(BF16)
    return high, low


def split3(value):
    high = value.astype(BF16)
    rest = value - high.astype(F32)
    middle = rest.astype(BF16)
    low = (rest - middle.astype(F32)).astype(BF16)
    return high, middle, low


def column_groups(groups, width):
    best = 1
    for count in range(1, groups + 1):
        if groups % count == 0 and width % count == 0 and (width // count) % 8 == 0:
            best = count
    return best


def hot_t(row, levels):
    return jnp.where(levels == row, jnp.ones((), BF16), jnp.zeros((), BF16))


def flip(value, mask, size):
    total, digit = 0, 1
    while digit < size:
        total = total + digit * lax.rem(value // digit + mask // digit, 2)
        digit *= 2
    return total


def column(pieces):
    total = pieces[0]
    for piece in pieces[1:]:
        total = total + piece
    return jnp.sum(total, axis=1, keepdims=True)


def kernel(n, nblk, ncg, ridge_ref, codes_ref, weights_ref, vectors_ref, book_out, residual_out, sum_out,
           mass_ref, codes_all, mass_all, part, pieces, gram, halves, swap, solution, remain, direction, inverse,
           books, parts, gathered, send_sem, recv_sem, swap_send, swap_recv, far_send, far_recv,
           near_send, near_recv, sum_send, sum_recv, pass_send, pass_recv):
    width, rows = vectors_ref.shape
    gsz = M // nblk
    cols = width // ncg
    me = lax.axis_index("dp")
    blk = lax.axis_index("blk")
    group, member = me // gsz, lax.rem(me, gsz)
    book = nblk * member + blk
    mine = lax.rem(group, ncg)
    bases = group - mine
    half = M // nblk
    peers = [(dm, db) for dm in range(gsz - 1, -1, -1) for db in range(nblk - 1, -1, -1) if (dm, db) != (0, 0)]

    def chip(k):
        return {"dp": flip(me, k, n)}

    def team(dm, db):
        return {"dp": group * gsz + flip(member, dm, gsz), "blk": lax.rem(blk + db, nblk)}

    def far(k):
        return {"dp": (bases + lax.rem(mine + k, ncg)) * gsz + member, "blk": blk}

    def remote(source, target, send, recv, to):
        return pltpu.make_async_remote_copy(
            src_ref=source, dst_ref=target, send_sem=send, recv_sem=recv, device_id=to, device_id_type=MESH
        )

    def loop(function):
        def step(k, carry):
            function(k)
            return carry

        lax.fori_loop(1, n, step, 0)

    barrier = pltpu.get_barrier_semaphore()
    mass_ref[...] = weights_ref[...].astype(F32).reshape(1, rows)
    loop(lambda k: pl.semaphore_signal(barrier, inc=1, device_id=chip(k), device_id_type=MESH))
    others = [(dm, db) for dm, db in peers if db]
    for dm, db in others:
        pl.semaphore_signal(barrier, inc=1, device_id=team(dm, db), device_id_type=MESH)

    triple = jnp.concatenate(split3(vectors_ref[...]), axis=0)
    levels = lax.broadcasted_iota(jnp.int32, (K, rows), 0).astype(F32).astype(BF16)

    def spread(row, mass):
        return jnp.where(levels == row.astype(F32).astype(BF16), jnp.broadcast_to(mass, (K, rows)), jnp.zeros((), BF16))

    for m in range(gsz):
        hot = spread(codes_ref[pl.ds(nblk * m + blk, 1), :], mass_ref[...].astype(BF16))
        sums = lax.dot_general(triple, hot, NT, preferred_element_type=F32)
        total = sums[:width] + sums[width : 2 * width] + sums[2 * width :]
        for c in range(ncg):
            part[c, m] = total[c * cols : (c + 1) * cols]
    pl.semaphore_wait(barrier, n - 1 + len(others))

    share = rows // nblk
    lanes = pl.ds(pl.multiple_of(blk * share, share), share)

    def codes_copy(k):
        source, target = codes_ref.at[:, lanes], codes_all.at[me, :, lanes]
        return remote(source, target, send_sem.at[0, k], recv_sem.at[0, k], chip(k))

    def mass_copy(k):
        source, target = mass_ref.at[:, lanes], mass_all.at[me, :, lanes]
        return remote(source, target, send_sem.at[1, k], recv_sem.at[1, k], chip(k))

    def passes(k):
        there = chip(k)["dp"]
        copies = []
        for db in range(1, nblk):
            for i, array in enumerate((codes_all, mass_all)):
                piece = array.at[there, :, lanes]
                to = {"blk": lax.rem(blk + db, nblk)}
                copies.append(remote(piece, piece, pass_send.at[i, db, k], pass_recv.at[i, db, k], to))
        return copies

    def pass_on(k):
        codes_copy(k).wait_recv()
        mass_copy(k).wait_recv()
        for copy in passes(k):
            copy.start()

    def piece_copy(k):
        to = chip(k)["dp"]
        piece = part.at[lax.rem(to // gsz, ncg), lax.rem(to, gsz)]
        return remote(piece, pieces.at[me], send_sem.at[2, k], recv_sem.at[2, k], chip(k))

    def send_codes(k):
        codes_copy(k).start()
        mass_copy(k).start()

    loop(send_codes)

    codes_all[me] = codes_ref[...]
    mass_all[me] = mass_ref[...]
    pieces[me] = part[mine, member]
    gram[...] = jnp.zeros_like(gram)

    def block(q):
        return pl.ds(pl.multiple_of(q * K, K), K)

    def accumulate(source):
        weighted = spread(codes_all[source, pl.ds(book, 1), :], mass_all[source].astype(BF16))
        for j in range(1, M):
            other = lax.rem(book + j, M)
            hot = spread(codes_all[source, pl.ds(other, 1), :], jnp.ones((1, 1), BF16))
            gram[block(other), :] += lax.dot_general(hot, weighted, NT, preferred_element_type=F32)

    accumulate(me)
    pass_on(1)

    def arrive(k):
        piece_copy(k).start()
        for copy in passes(k):
            copy.wait_recv()

        @pl.when(k + 1 < n)
        def _():
            pass_on(k + 1)

        accumulate(chip(k)["dp"])

    loop(arrive)

    square = (K, K)
    own = jnp.sum(gram[block(lax.rem(book + 1, M)), :], axis=0, keepdims=True)
    diagonal = lax.broadcasted_iota(jnp.int32, square, 0) == lax.broadcasted_iota(jnp.int32, square, 1)
    gram[block(book), :] = jnp.where(diagonal, jnp.broadcast_to(own, square), 0.0)
    ones = jnp.ones((8, K), F32)
    for q in range(M):
        value = gram[block(q), :]
        high, low = split2(value)
        halves[block(q), :K] = high
        halves[block(q), K:] = low
        inverse[q] = lax.dot_general(ones, value, NT, precision=HIGH, preferred_element_type=F32)
    whole = jnp.sum(inverse[0, 0:1, :])
    lam = ridge_ref[0] * (whole / K)
    for q in range(M):
        inverse[q] = 1.0 / (inverse[q] + lam)

    loop(lambda k: piece_copy(k).wait_recv())
    right = lax.fori_loop(1, n, lambda s, total: total + pieces[s], pieces[0])

    streams = [(i, pl.ds(first, last - first), last - first) for i, (first, last) in enumerate([(c, c + 8) for c in range(0, cols, 8)])]

    def copies(stream, slot):
        i, span, _ = stream
        here = swap.at[slot, book, span]
        return [
            remote(here, here, swap_send.at[slot, i, j], swap_recv.at[slot, i, j], team(dm, db))
            for j, (dm, db) in enumerate(peers)
        ]

    def send(stream, slot, value):
        swap[slot, book, stream[1]] = value
        for copy in copies(stream, slot):
            copy.start()

    def receive(stream, slot):
        for copy in copies(stream, slot):
            copy.wait()

    def apply(stream):
        _, span, size = stream
        product = None
        for q in range(M):
            left = jnp.concatenate(split2(direction[q, span]), axis=0)
            term = jnp.dot(left, halves[pl.ds(q * K, K), :], preferred_element_type=F32)
            product = term if product is None else product + term
        return (product[:size, :K] + product[size:, :K]) + (product[:size, K:] + product[size:, K:])

    def begin(stream):
        _, span, _ = stream
        receive(stream, 0)
        terms = []
        for q in range(M):
            r = swap[0, q, span]
            z = r * inverse[q, 0:1, :]
            remain[q, span] = r
            direction[q, span] = z
            solution[q, span] = jnp.zeros_like(r)
            terms.append(r * z)
        send(stream, 1, apply(stream))
        return column(terms)

    def advance(stream, slot, inner):
        _, span, _ = stream
        receive(stream, slot)
        terms = []
        for q in range(M):
            d = direction[q, span]
            terms.append(d * (swap[slot, q, span] + lam * d))
        alpha = inner / column(terms)
        terms = []
        for q in range(M):
            d = direction[q, span]
            r = remain[q, span] - alpha * (swap[slot, q, span] + lam * d)
            solution[q, span] = solution[q, span] + alpha * d
            remain[q, span] = r
            terms.append(r * (r * inverse[q, 0:1, :]))
        fresh = column(terms)
        beta = fresh / inner
        for q in range(M):
            direction[q, span] = remain[q, span] * inverse[q, 0:1, :] + beta * direction[q, span]
        return fresh

    def iterate(step, inners):
        slot = lax.rem(step, 2)
        results = []
        for stream, inner in zip(streams, inners):
            results.append(advance(stream, slot, inner))
            send(stream, 1 - slot, apply(stream))
        return tuple(results)

    for stream in streams:
        first = stream[1].start
        send(stream, 0, right[first : first + stream[2]])
    inners = lax.fori_loop(1, ITERS, iterate, tuple(begin(stream) for stream in streams))
    for stream, inner in zip(streams, inners):
        advance(stream, ITERS % 2, inner)

    span = pl.ds(blk * half, half)
    away = [
        remote(solution.at[span], books.at[mine, span], far_send.at[k], far_recv.at[k], far(k)) for k in range(1, ncg)
    ]
    for copy in away:
        copy.start()
    for q in range(M):
        books[mine, q] = solution[q]
    relays = []
    for k in range(1, ncg):
        away[k - 1].wait_recv()
        there = books.at[lax.rem(mine - k + ncg, ncg), span]
        for db in range(1, nblk):
            relay = remote(there, there, near_send.at[k, db], near_recv.at[k, db], team(0, db))
            relay.start()
            relays.append(relay)
    for relay in relays:
        relay.wait()

    for q in range(M):
        value = jnp.concatenate([books[c, q] for c in range(ncg)], axis=0)
        book_out[q] = value
        high, low = split2(value)
        parts[q, :width, :] = high
        parts[q, width:, :] = low

    size = min(256, rows)
    short = lax.broadcasted_iota(jnp.int32, (K, size), 0).astype(F32).astype(BF16)

    def rebuild(turn, total):
        at = pl.ds(pl.multiple_of(turn * size, size), size)
        value = jnp.zeros((2 * width, size), F32)
        for q in range(M):
            row = codes_ref[q : q + 1, at].astype(F32).astype(BF16)
            value = value + jnp.dot(parts[q], hot_t(row, short), preferred_element_type=F32)
        residual = vectors_ref[:, at] - (value[:width] + value[width:])
        residual_out[:, at] = residual
        return total + mass_ref[:, at] * (residual * residual)

    total = lax.fori_loop(0, rows // size, rebuild, jnp.zeros((width, size), F32))
    gathered[me] = jnp.broadcast_to(jnp.sum(total, keepdims=True), (8, 128))

    def sum_copy(k):
        return remote(gathered.at[me], gathered.at[me], sum_send.at[k], sum_recv.at[k], chip(k))

    loop(lambda k: sum_copy(k).start())
    for copy in away:
        copy.wait_send()

    def drain(k):
        codes_copy(k).wait_send()
        mass_copy(k).wait_send()
        piece_copy(k).wait_send()
        for copy in passes(k):
            copy.wait_send()

    loop(drain)
    loop(lambda k: sum_copy(k).wait())
    final = lax.fori_loop(1, n, lambda s, value: value + gathered[s], gathered[0])
    sum_out[...] = final / (whole * width)


def store(books_ref, residual_ref, sum_ref, books_out, residual_out, sum_out, sems):
    copies = [
        pltpu.make_async_copy(books_ref, books_out, sems.at[0]),
        pltpu.make_async_copy(residual_ref, residual_out, sems.at[1]),
    ]
    for copy in copies:
        copy.start()
    sum_out[...] = sum_ref[0:1, 0:1]
    for copy in copies:
        copy.wait()


def body(vectors, codes, weights, ridge):
    rows, width = vectors.shape
    n, nblk = lax.axis_size("dp"), lax.axis_size("blk")
    gsz = M // nblk
    ncg = column_groups(n // gsz, width)
    cols = width // ncg
    shape = jax.ShapeDtypeStruct
    dma = pltpu.SemaphoreType.DMA
    state = pltpu.VMEM((M, cols, K), F32)
    books, residual, distortion = pl.pallas_call(
        functools.partial(kernel, n, nblk, ncg),
        out_shape=(pltpu.VMEM((M, width, K), F32), pltpu.VMEM((width, rows), F32), pltpu.VMEM((8, 128), F32)),
        in_specs=[pl.BlockSpec(memory_space=pltpu.SMEM)] + [vmem()] * 3,
        out_specs=(vmem(),) * 3,
        scratch_shapes=[
            pltpu.VMEM((1, rows), F32),
            pltpu.VMEM((n, M, rows), jnp.int32),
            pltpu.VMEM((n, 1, rows), F32),
            pltpu.VMEM((ncg, gsz, cols, K), F32),
            pltpu.VMEM((n, cols, K), F32),
            pltpu.VMEM((M * K, K), F32),
            pltpu.VMEM((M * K, 2 * K), BF16),
            pltpu.VMEM((2, M, cols, K), F32),
            state,
            state,
            state,
            pltpu.VMEM((M, 8, K), F32),
            pltpu.VMEM((ncg, M, cols, K), F32),
            pltpu.VMEM((M, 2 * width, K), BF16),
            pltpu.VMEM((n, 8, 128), F32),
            dma((3, n)),
            dma((3, n)),
            dma((2, 3, M)),
            dma((2, 3, M)),
            dma((ncg,)),
            dma((ncg,)),
            dma((ncg, nblk)),
            dma((ncg, nblk)),
            dma((n,)),
            dma((n,)),
            dma((2, nblk, n)),
            dma((2, nblk, n)),
        ],
        compiler_params=pltpu.CompilerParams(collective_id=0, has_side_effects=True),
        name="update",
    )(ridge, codes.T, weights, vectors.T)
    books, residual, distortion = pl.pallas_call(
        store,
        out_shape=(shape((M, width, K), F32), shape((width, rows), F32), shape((1, 1), F32)),
        in_specs=[vmem()] * 3,
        out_specs=(pl.BlockSpec(memory_space=pl.ANY), pl.BlockSpec(memory_space=pl.ANY), vmem()),
        scratch_shapes=[dma((2,))],
        name="store",
    )(*(pltpu.with_memory_space_constraint(value, pltpu.VMEM) for value in (books, residual, distortion)))
    return (books.transpose(0, 2, 1), residual.T, distortion[0, 0])


def solution(mesh):
    return jax.shard_map(
        body,
        mesh=mesh,
        in_specs=(P("dp", None), P("dp", None), P("dp"), P()),
        out_specs=(P(), P("dp", None), P()),
        check_vma=False,
    )
```

```python
import functools

import jax
import jax.numpy as jnp
from jax import lax
from jax.experimental import pallas as pl
from jax.experimental.pallas import tpu as pltpu
from jax.sharding import PartitionSpec as P

K = 256
M = 8
ITERS = 8
MESH = pl.DeviceIdType.MESH
HIGH = lax.Precision.HIGHEST
F32 = jnp.float32
BF16 = jnp.bfloat16
NT = (((1,), (1,)), ((), ()))


def vmem():
    return pl.BlockSpec(memory_space=pltpu.VMEM)


def split2(value):
    high = value.astype(BF16)
    low = (value - high.astype(F32)).astype(BF16)
    return high, low


def split3(value):
    high = value.astype(BF16)
    rest = value - high.astype(F32)
    middle = rest.astype(BF16)
    low = (rest - middle.astype(F32)).astype(BF16)
    return high, middle, low


def column_groups(groups, width):
    best = 1
    for count in range(1, groups + 1):
        if groups % count == 0 and width % count == 0 and (width // count) % 8 == 0:
            best = count
    return best


def hot_t(row, levels):
    return jnp.where(levels == row, jnp.ones((), BF16), jnp.zeros((), BF16))


def flip(value, mask, size):
    total, digit = 0, 1
    while digit < size:
        total = total + digit * lax.rem(value // digit + mask // digit, 2)
        digit *= 2
    return total


def column(pieces):
    total = pieces[0]
    for piece in pieces[1:]:
        total = total + piece
    return jnp.sum(total, axis=1, keepdims=True)


def kernel(n, nblk, ncg, ridge_ref, codes_ref, weights_ref, vectors_ref, book_out, residual_out, sum_out,
           mass_ref, codes_all, mass_all, part, pieces, gram, halves, swap, solution, remain, direction, inverse,
           books, parts, gathered, send_sem, recv_sem, swap_send, swap_recv, far_send, far_recv,
           near_send, near_recv, sum_send, sum_recv, pass_send, pass_recv, crew, team_parts, pairs,
           team_send, team_recv, pair_send, pair_recv):
    width, rows = vectors_ref.shape
    gsz = M // nblk
    cols = width // ncg
    me = lax.axis_index("dp")
    blk = lax.axis_index("blk")
    group, member = me // gsz, lax.rem(me, gsz)
    book = nblk * member + blk
    mine = lax.rem(group, ncg)
    bases = group - mine
    half = M // nblk
    peers = [(dm, db) for dm in range(gsz - 1, -1, -1) for db in range(nblk - 1, -1, -1) if (dm, db) != (0, 0)]

    def chip(k):
        return {"dp": flip(me, k, n)}

    def team(dm, db):
        return {"dp": group * gsz + flip(member, dm, gsz), "blk": lax.rem(blk + db, nblk)}

    def far(k):
        return {"dp": (bases + lax.rem(mine + k, ncg)) * gsz + member, "blk": blk}

    def remote(source, target, send, recv, to):
        return pltpu.make_async_remote_copy(
            src_ref=source, dst_ref=target, send_sem=send, recv_sem=recv, device_id=to, device_id_type=MESH
        )

    def loop(function):
        def step(k, carry):
            function(k)
            return carry

        lax.fori_loop(1, n, step, 0)

    barrier = pltpu.get_barrier_semaphore()
    mass_ref[...] = weights_ref[...].astype(F32).reshape(1, rows)
    loop(lambda k: pl.semaphore_signal(barrier, inc=1, device_id=chip(k), device_id_type=MESH))
    others = [(dm, db) for dm, db in peers if db]
    for dm, db in others:
        pl.semaphore_signal(barrier, inc=1, device_id=team(dm, db), device_id_type=MESH)

    triple = jnp.concatenate(split3(vectors_ref[...]), axis=0)
    levels = lax.broadcasted_iota(jnp.int32, (K, rows), 0).astype(F32).astype(BF16)

    def spread(row, mass):
        return jnp.where(levels == row.astype(F32).astype(BF16), jnp.broadcast_to(mass, (K, rows)), jnp.zeros((), BF16))

    for m in range(gsz):
        hot = spread(codes_ref[pl.ds(nblk * m + blk, 1), :], mass_ref[...].astype(BF16))
        sums = lax.dot_general(triple, hot, NT, preferred_element_type=F32)
        total = sums[:width] + sums[width : 2 * width] + sums[2 * width :]
        for c in range(ncg):
            part[c, m] = total[c * cols : (c + 1) * cols]
    pl.semaphore_wait(barrier, n - 1 + len(others))

    share = rows // nblk
    lanes = pl.ds(pl.multiple_of(blk * share, share), share)

    def codes_copy(k):
        source, target = codes_ref.at[:, lanes], codes_all.at[me, :, lanes]
        return remote(source, target, send_sem.at[0, k], recv_sem.at[0, k], chip(k))

    def mass_copy(k):
        source, target = mass_ref.at[:, lanes], mass_all.at[me, :, lanes]
        return remote(source, target, send_sem.at[1, k], recv_sem.at[1, k], chip(k))

    def passes(k):
        there = chip(k)["dp"]
        copies = []
        for db in range(1, nblk):
            for i, array in enumerate((codes_all, mass_all)):
                piece = array.at[there, :, lanes]
                to = {"blk": lax.rem(blk + db, nblk)}
                copies.append(remote(piece, piece, pass_send.at[i, db, k], pass_recv.at[i, db, k], to))
        return copies

    def pass_on(k):
        codes_copy(k).wait_recv()
        mass_copy(k).wait_recv()
        for copy in passes(k):
            copy.start()

    def piece_copy(k):
        to = chip(k)["dp"]
        piece = part.at[lax.rem(to // gsz, ncg), lax.rem(to, gsz)]
        return remote(piece, pieces.at[me], send_sem.at[2, k], recv_sem.at[2, k], chip(k))

    def send_codes(k):
        codes_copy(k).start()
        mass_copy(k).start()

    loop(send_codes)

    codes_all[me] = codes_ref[...]
    mass_all[me] = mass_ref[...]
    pieces[me] = part[mine, member]
    gram[...] = jnp.zeros_like(gram)

    def block(q):
        return pl.ds(pl.multiple_of(q * K, K), K)

    def accumulate(source):
        weighted = spread(codes_all[source, pl.ds(book, 1), :], mass_all[source].astype(BF16))
        for j in range(1, M):
            other = lax.rem(book + j, M)
            hot = spread(codes_all[source, pl.ds(other, 1), :], jnp.ones((1, 1), BF16))
            gram[block(other), :] += lax.dot_general(hot, weighted, NT, preferred_element_type=F32)

    accumulate(me)
    pass_on(1)

    def arrive(k):
        piece_copy(k).start()
        for copy in passes(k):
            copy.wait_recv()

        @pl.when(k + 1 < n)
        def _():
            pass_on(k + 1)

        accumulate(chip(k)["dp"])

    loop(arrive)

    square = (K, K)
    own = jnp.sum(gram[block(lax.rem(book + 1, M)), :], axis=0, keepdims=True)
    diagonal = lax.broadcasted_iota(jnp.int32, square, 0) == lax.broadcasted_iota(jnp.int32, square, 1)
    gram[block(book), :] = jnp.where(diagonal, jnp.broadcast_to(own, square), 0.0)
    ones = jnp.ones((8, K), F32)
    for q in range(M):
        value = gram[block(q), :]
        high, low = split2(value)
        halves[block(q), :K] = high
        halves[block(q), K:] = low
        inverse[q] = lax.dot_general(ones, value, NT, precision=HIGH, preferred_element_type=F32)
    whole = jnp.sum(inverse[0, 0:1, :])
    lam = ridge_ref[0] * (whole / K)
    for q in range(M):
        inverse[q] = 1.0 / (inverse[q] + lam)

    loop(lambda k: piece_copy(k).wait_recv())
    right = lax.fori_loop(1, n, lambda s, total: total + pieces[s], pieces[0])

    def band(c):
        return pl.ds(pl.multiple_of(c * cols, 8), cols)

    def team_copy(k):
        source, target = vectors_ref.at[band(lax.rem(mine + k, ncg)), lanes], crew.at[mine]
        return remote(source, target, team_send.at[k], team_recv.at[k], far(k))

    for k in range(1, ncg):
        team_copy(k).start()
    crew[mine] = vectors_ref[band(mine), lanes]

    streams = [(i, pl.ds(first, last - first), last - first) for i, (first, last) in enumerate([(c, c + 8) for c in range(0, cols, 8)])]

    def copies(stream, slot):
        i, span, _ = stream
        here = swap.at[slot, book, span]
        return [
            remote(here, here, swap_send.at[slot, i, j], swap_recv.at[slot, i, j], team(dm, db))
            for j, (dm, db) in enumerate(peers)
        ]

    def send(stream, slot, value):
        swap[slot, book, stream[1]] = value
        for copy in copies(stream, slot):
            copy.start()

    def receive(stream, slot):
        for copy in copies(stream, slot):
            copy.wait()

    def apply(stream):
        _, span, size = stream
        product = None
        for q in range(M):
            left = jnp.concatenate(split2(direction[q, span]), axis=0)
            term = jnp.dot(left, halves[pl.ds(q * K, K), :], preferred_element_type=F32)
            product = term if product is None else product + term
        return (product[:size, :K] + product[size:, :K]) + (product[:size, K:] + product[size:, K:])

    def begin(stream):
        _, span, _ = stream
        receive(stream, 0)
        terms = []
        for q in range(M):
            r = swap[0, q, span]
            z = r * inverse[q, 0:1, :]
            remain[q, span] = r
            direction[q, span] = z
            solution[q, span] = jnp.zeros_like(r)
            terms.append(r * z)
        send(stream, 1, apply(stream))
        return column(terms)

    def advance(stream, slot, inner):
        _, span, _ = stream
        receive(stream, slot)
        terms = []
        for q in range(M):
            d = direction[q, span]
            terms.append(d * (swap[slot, q, span] + lam * d))
        alpha = inner / column(terms)
        terms = []
        for q in range(M):
            d = direction[q, span]
            r = remain[q, span] - alpha * (swap[slot, q, span] + lam * d)
            solution[q, span] = solution[q, span] + alpha * d
            remain[q, span] = r
            terms.append(r * (r * inverse[q, 0:1, :]))
        fresh = column(terms)
        beta = fresh / inner
        for q in range(M):
            direction[q, span] = remain[q, span] * inverse[q, 0:1, :] + beta * direction[q, span]
        return fresh

    def iterate(step, inners):
        slot = lax.rem(step, 2)
        results = []
        for stream, inner in zip(streams, inners):
            results.append(advance(stream, slot, inner))
            send(stream, 1 - slot, apply(stream))
        return tuple(results)

    for stream in streams:
        first = stream[1].start
        send(stream, 0, right[first : first + stream[2]])
    inners = lax.fori_loop(1, ITERS, iterate, tuple(begin(stream) for stream in streams))
    span = pl.ds(blk * half, half)

    def away(stream, k):
        i, place, _ = stream
        source, target = solution.at[span, place], books.at[mine, span, place]
        return remote(source, target, far_send.at[i, k], far_recv.at[i, k], far(k))

    for stream, inner in zip(streams, inners):
        advance(stream, ITERS % 2, inner)
        for k in range(1, ncg):
            away(stream, k).start()

    for q in range(M):
        value = solution[q]
        books[mine, q] = value
        high = value.astype(BF16).astype(F32)
        team_parts[q] = jnp.concatenate([high, value - high], axis=0).astype(BF16)
    for k in range(1, ncg):
        team_copy(k).wait()
    size = min(256, share)
    short = lax.broadcasted_iota(jnp.int32, (K, size), 0).astype(F32).astype(BF16)

    def squares(turn, total):
        c, first = lax.div(turn, share // size), lax.rem(turn, share // size) * size
        source = (bases + c) * gsz + member
        at = pl.ds(pl.multiple_of(blk * share + first, size), size)
        value = jnp.zeros((2 * cols, size), F32)
        for q in range(M):
            row = codes_all[source, q : q + 1, at].astype(F32).astype(BF16)
            value = value + jnp.dot(team_parts[q], hot_t(row, short), preferred_element_type=F32)
        residual = crew[c, :, pl.ds(pl.multiple_of(first, size), size)] - (value[:cols] + value[cols:])
        return total + mass_all[source, :, at] * (residual * residual)

    total = lax.fori_loop(0, ncg * (share // size), squares, jnp.zeros((cols, size), F32))
    pairs[blk] = jnp.broadcast_to(jnp.sum(total, keepdims=True), (8, 128))
    beside = [
        remote(pairs.at[blk], pairs.at[blk], pair_send.at[db], pair_recv.at[db], {"blk": lax.rem(blk + db, nblk)})
        for db in range(1, nblk)
    ]
    for copy in beside:
        copy.start()
    for copy in beside:
        copy.wait()
    both = pairs[0]
    for b in range(1, nblk):
        both = both + pairs[b]
    gathered[me] = both

    def sum_copy(k):
        row = gathered.at[me, pl.ds(0, 1)]
        return remote(row, row, sum_send.at[k], sum_recv.at[k], chip(k))

    loop(lambda k: sum_copy(k).start())

    relays = []
    for stream in streams:
        i, place, _ = stream
        for k in range(1, ncg):
            away(stream, k).wait_recv()
            there = books.at[lax.rem(mine - k + ncg, ncg), span, place]
            for db in range(1, nblk):
                relay = remote(there, there, near_send.at[i, k, db], near_recv.at[i, k, db], team(0, db))
                relay.start()
                relays.append(relay)
    for relay in relays:
        relay.wait()

    for q in range(M):
        value = jnp.concatenate([books[c, q] for c in range(ncg)], axis=0)
        book_out[q] = value
        high, low = split2(value)
        parts[q, :width, :] = high
        parts[q, width:, :] = low

    def rebuild(turn):
        at = pl.ds(pl.multiple_of(turn * size, size), size)
        value = jnp.zeros((2 * width, size), F32)
        for q in range(M):
            row = codes_ref[q : q + 1, at].astype(F32).astype(BF16)
            value = value + jnp.dot(parts[q], hot_t(row, short), preferred_element_type=F32)
        residual_out[:, at] = vectors_ref[:, at] - (value[:width] + value[width:])

    pl.loop(0, rows // size)(rebuild)
    for stream in streams:
        for k in range(1, ncg):
            away(stream, k).wait_send()

    def drain(k):
        codes_copy(k).wait_send()
        mass_copy(k).wait_send()
        piece_copy(k).wait_send()
        for copy in passes(k):
            copy.wait_send()

    loop(drain)
    loop(lambda k: sum_copy(k).wait())
    final = lax.fori_loop(1, n, lambda s, value: value + gathered[s, 0:1], gathered[0, 0:1])
    sum_out[...] = jnp.broadcast_to(final / (whole * width), (8, 128))


def store(books_ref, residual_ref, sum_ref, books_out, residual_out, sum_out, sems):
    copies = [
        pltpu.make_async_copy(books_ref, books_out, sems.at[0]),
        pltpu.make_async_copy(residual_ref, residual_out, sems.at[1]),
    ]
    for copy in copies:
        copy.start()
    sum_out[...] = sum_ref[0:1, 0:1]
    for copy in copies:
        copy.wait()


def body(vectors, codes, weights, ridge):
    rows, width = vectors.shape
    n, nblk = lax.axis_size("dp"), lax.axis_size("blk")
    gsz = M // nblk
    ncg = column_groups(n // gsz, width)
    cols = width // ncg
    shape = jax.ShapeDtypeStruct
    dma = pltpu.SemaphoreType.DMA
    state = pltpu.VMEM((M, cols, K), F32)
    books, residual, distortion = pl.pallas_call(
        functools.partial(kernel, n, nblk, ncg),
        out_shape=(pltpu.VMEM((M, width, K), F32), pltpu.VMEM((width, rows), F32), pltpu.VMEM((8, 128), F32)),
        in_specs=[pl.BlockSpec(memory_space=pltpu.SMEM)] + [vmem()] * 3,
        out_specs=(vmem(),) * 3,
        scratch_shapes=[
            pltpu.VMEM((1, rows), F32),
            pltpu.VMEM((n, M, rows), jnp.int32),
            pltpu.VMEM((n, 1, rows), F32),
            pltpu.VMEM((ncg, gsz, cols, K), F32),
            pltpu.VMEM((n, cols, K), F32),
            pltpu.VMEM((M * K, K), F32),
            pltpu.VMEM((M * K, 2 * K), BF16),
            pltpu.VMEM((2, M, cols, K), F32),
            state,
            state,
            state,
            pltpu.VMEM((M, 8, K), F32),
            pltpu.VMEM((ncg, M, cols, K), F32),
            pltpu.VMEM((M, 2 * width, K), BF16),
            pltpu.VMEM((n, 8, 128), F32),
            dma((3, n)),
            dma((3, n)),
            dma((2, 3, M)),
            dma((2, 3, M)),
            dma((cols // 8, ncg)),
            dma((cols // 8, ncg)),
            dma((cols // 8, ncg, nblk)),
            dma((cols // 8, ncg, nblk)),
            dma((n,)),
            dma((n,)),
            dma((2, nblk, n)),
            dma((2, nblk, n)),
            pltpu.VMEM((ncg, cols, rows // nblk), F32),
            pltpu.VMEM((M, 2 * cols, K), BF16),
            pltpu.VMEM((nblk, 8, 128), F32),
            dma((ncg,)),
            dma((ncg,)),
            dma((nblk,)),
            dma((nblk,)),
        ],
        compiler_params=pltpu.CompilerParams(collective_id=0, has_side_effects=True),
        name="update",
    )(ridge, codes.T, weights, vectors.T)
    books, residual, distortion = pl.pallas_call(
        store,
        out_shape=(shape((M, width, K), F32), shape((width, rows), F32), shape((1, 1), F32)),
        in_specs=[vmem()] * 3,
        out_specs=(pl.BlockSpec(memory_space=pl.ANY), pl.BlockSpec(memory_space=pl.ANY), vmem()),
        scratch_shapes=[dma((2,))],
        name="store",
    )(*(pltpu.with_memory_space_constraint(value, pltpu.VMEM) for value in (books, residual, distortion)))
    return (books.transpose(0, 2, 1), residual.T, distortion[0, 0])


def solution(mesh):
    return jax.shard_map(
        body,
        mesh=mesh,
        in_specs=(P("dp", None), P("dp", None), P("dp"), P()),
        out_specs=(P(), P("dp", None), P()),
        check_vma=False,
    )
```

```python
import functools

import jax
import jax.numpy as jnp
from jax import lax
from jax.experimental import pallas as pl
from jax.experimental.pallas import tpu as pltpu
from jax.sharding import PartitionSpec as P

K = 256
M = 8
ITERS = 8
LATE = 3
MESH = pl.DeviceIdType.MESH
HIGH = lax.Precision.HIGHEST
F32 = jnp.float32
BF16 = jnp.bfloat16
NT = (((1,), (1,)), ((), ()))


def vmem():
    return pl.BlockSpec(memory_space=pltpu.VMEM)


def split2(value):
    high = value.astype(BF16)
    low = (value - high.astype(F32)).astype(BF16)
    return high, low


def split3(value):
    high = value.astype(BF16)
    rest = value - high.astype(F32)
    middle = rest.astype(BF16)
    low = (rest - middle.astype(F32)).astype(BF16)
    return high, middle, low


def column_groups(groups, width):
    best = 1
    for count in range(1, groups + 1):
        if groups % count == 0 and width % count == 0 and (width // count) % 8 == 0:
            best = count
    return best


def hot_t(row, levels):
    return jnp.where(levels == row, jnp.ones((), BF16), jnp.zeros((), BF16))


def flip(value, mask, size):
    total, digit = 0, 1
    while digit < size:
        total = total + digit * lax.rem(value // digit + mask // digit, 2)
        digit *= 2
    return total


def column(pieces):
    total = pieces[0]
    for piece in pieces[1:]:
        total = total + piece
    return jnp.sum(total, axis=1, keepdims=True)


def kernel(n, nblk, ncg, ridge_ref, codes_ref, weights_ref, vectors_ref, book_out, residual_out, sum_out,
           mass_ref, codes_all, mass_all, part, pieces, gram, halves, swap, solution, remain, direction, inverse,
           books, parts, gathered, send_sem, recv_sem, swap_send, swap_recv, far_send, far_recv,
           near_send, near_recv, sum_send, sum_recv, pass_send, pass_recv, counts, crew, team_parts, pairs,
           team_send, team_recv, pair_send, pair_recv):
    width, rows = vectors_ref.shape
    gsz = M // nblk
    cols = width // ncg
    me = lax.axis_index("dp")
    blk = lax.axis_index("blk")
    group, member = me // gsz, lax.rem(me, gsz)
    book = nblk * member + blk
    mine = lax.rem(group, ncg)
    bases = group - mine
    half = M // nblk
    peers = [(dm, db) for dm in range(gsz - 1, -1, -1) for db in range(nblk - 1, -1, -1) if (dm, db) != (0, 0)]

    def chip(k):
        return {"dp": flip(me, k, n)}

    def team(dm, db):
        return {"dp": group * gsz + flip(member, dm, gsz), "blk": lax.rem(blk + db, nblk)}

    def far(k):
        return {"dp": (bases + lax.rem(mine + k, ncg)) * gsz + member, "blk": blk}

    def remote(source, target, send, recv, to):
        return pltpu.make_async_remote_copy(
            src_ref=source, dst_ref=target, send_sem=send, recv_sem=recv, device_id=to, device_id_type=MESH
        )

    def loop(function):
        def step(k, carry):
            function(k)
            return carry

        lax.fori_loop(1, n, step, 0)

    barrier = pltpu.get_barrier_semaphore()
    mass_ref[...] = weights_ref[...].astype(F32).reshape(1, rows)
    loop(lambda k: pl.semaphore_signal(barrier, inc=1, device_id=chip(k), device_id_type=MESH))
    others = [(dm, db) for dm, db in peers if db]
    for dm, db in others:
        pl.semaphore_signal(barrier, inc=1, device_id=team(dm, db), device_id_type=MESH)

    triple = jnp.concatenate(split3(vectors_ref[...]), axis=0)
    levels = lax.broadcasted_iota(jnp.int32, (K, rows), 0).astype(F32).astype(BF16)

    def spread(row, mass):
        return jnp.where(levels == row.astype(F32).astype(BF16), jnp.broadcast_to(mass, (K, rows)), jnp.zeros((), BF16))

    for m in range(gsz):
        hot = spread(codes_ref[pl.ds(nblk * m + blk, 1), :], mass_ref[...].astype(BF16))
        sums = lax.dot_general(triple, hot, NT, preferred_element_type=F32)
        total = sums[:width] + sums[width : 2 * width] + sums[2 * width :]
        for c in range(ncg):
            part[c, m] = total[c * cols : (c + 1) * cols]
    pl.semaphore_wait(barrier, n - 1 + len(others))

    share = rows // nblk
    lanes = pl.ds(pl.multiple_of(blk * share, share), share)

    def codes_copy(k):
        source, target = codes_ref.at[:, lanes], codes_all.at[me, :, lanes]
        return remote(source, target, send_sem.at[0, k], recv_sem.at[0, k], chip(k))

    def mass_copy(k):
        source, target = mass_ref.at[:, lanes], mass_all.at[me, :, lanes]
        return remote(source, target, send_sem.at[1, k], recv_sem.at[1, k], chip(k))

    def passes(k):
        there = chip(k)["dp"]
        copies = []
        for db in range(1, nblk):
            for i, array in enumerate((codes_all, mass_all)):
                piece = array.at[there, :, lanes]
                to = {"blk": lax.rem(blk + db, nblk)}
                copies.append(remote(piece, piece, pass_send.at[i, db, k], pass_recv.at[i, db, k], to))
        return copies

    def pass_on(k):
        codes_copy(k).wait_recv()
        mass_copy(k).wait_recv()
        for copy in passes(k):
            copy.start()

    def piece_copy(k):
        to = chip(k)["dp"]
        piece = part.at[lax.rem(to // gsz, ncg), lax.rem(to, gsz)]
        return remote(piece, pieces.at[me], send_sem.at[2, k], recv_sem.at[2, k], chip(k))

    def send_codes(k):
        codes_copy(k).start()
        mass_copy(k).start()

    loop(send_codes)
    loop(lambda k: piece_copy(k).start())

    codes_all[me] = codes_ref[...]
    mass_all[me] = mass_ref[...]
    pieces[me] = part[mine, member]
    gram[...] = jnp.zeros_like(gram)

    def block(q):
        return pl.ds(pl.multiple_of(q * K, K), K)

    def accumulate(source):
        weighted = spread(codes_all[source, pl.ds(book, 1), :], mass_all[source].astype(BF16))
        for j in range(1, M):
            other = lax.rem(book + j, M)
            hot = spread(codes_all[source, pl.ds(other, 1), :], jnp.ones((1, 1), BF16))
            gram[block(other), :] += lax.dot_general(hot, weighted, NT, preferred_element_type=F32)

    accumulate(me)
    pass_on(1)

    streams = [(i, pl.ds(first, last - first), last - first) for i, (first, last) in enumerate([(c, c + 8) for c in range(0, cols, 8)])]

    def copies(stream, slot):
        i, span, _ = stream
        here = swap.at[slot, book, span]
        return [
            remote(here, here, swap_send.at[slot, i, j], swap_recv.at[slot, i, j], team(dm, db))
            for j, (dm, db) in enumerate(peers)
        ]

    def send(stream, slot, value):
        swap[slot, book, stream[1]] = value
        for copy in copies(stream, slot):
            copy.start()

    def open_streams():
        loop(lambda k: piece_copy(k).wait_recv())
        right = lax.fori_loop(1, n, lambda s, total: total + pieces[s], pieces[0])
        for stream in streams:
            first = stream[1].start
            send(stream, 0, right[first : first + stream[2]])

    def arrive(k):
        pl.when(k == max(n - LATE, 1))(open_streams)
        for copy in passes(k):
            copy.wait_recv()

        @pl.when(k + 1 < n)
        def _():
            pass_on(k + 1)

        accumulate(chip(k)["dp"])

    loop(arrive)

    own = jnp.sum(gram[block(lax.rem(book + 1, M)), :], axis=0, keepdims=True)
    inverse[book] = jnp.broadcast_to(own, (8, K))
    counts[...] = inverse[book]
    ones = jnp.ones((8, K), BF16)
    for j in range(1, M):
        other = lax.rem(book + j, M)
        high, low, rest = split3(gram[block(other), :])
        halves[block(other), :K] = high
        halves[block(other), K:] = low
        total = None
        for piece in (high, low, rest):
            term = lax.dot_general(ones, piece, NT, preferred_element_type=F32)
            total = term if total is None else total + term
        inverse[other] = total
    whole = jnp.sum(inverse[0, 0:1, :])
    lam = ridge_ref[0] * (whole / K)
    for q in range(M):
        inverse[q] = 1.0 / (inverse[q] + lam)

    def band(c):
        return pl.ds(pl.multiple_of(c * cols, 8), cols)

    def team_copy(k):
        source, target = vectors_ref.at[band(lax.rem(mine + k, ncg)), lanes], crew.at[mine]
        return remote(source, target, team_send.at[k], team_recv.at[k], far(k))

    for k in range(1, ncg):
        team_copy(k).start()
    crew[mine] = vectors_ref[band(mine), lanes]

    def receive(stream, slot):
        for copy in copies(stream, slot):
            copy.wait()

    def apply(stream):
        _, span, size = stream
        product = None
        for j in range(1, M):
            other = lax.rem(book + j, M)
            left = jnp.concatenate(split2(direction[other, span]), axis=0)
            term = jnp.dot(left, halves[block(other), :], preferred_element_type=F32)
            product = term if product is None else product + term
        total = (product[:size, :K] + product[size:, :K]) + (product[:size, K:] + product[size:, K:])
        return total + counts[0:1, :] * direction[book, span]

    def begin(stream):
        _, span, _ = stream
        receive(stream, 0)
        terms = []
        for q in range(M):
            r = swap[0, q, span]
            z = r * inverse[q, 0:1, :]
            remain[q, span] = r
            direction[q, span] = z
            solution[q, span] = jnp.zeros_like(r)
            terms.append(r * z)
        send(stream, 1, apply(stream))
        return column(terms)

    def advance(stream, slot, inner):
        _, span, _ = stream
        receive(stream, slot)
        terms = []
        for q in range(M):
            d = direction[q, span]
            terms.append(d * (swap[slot, q, span] + lam * d))
        alpha = inner / column(terms)
        terms = []
        for q in range(M):
            d = direction[q, span]
            r = remain[q, span] - alpha * (swap[slot, q, span] + lam * d)
            solution[q, span] = solution[q, span] + alpha * d
            remain[q, span] = r
            terms.append(r * (r * inverse[q, 0:1, :]))
        fresh = column(terms)
        beta = fresh / inner
        for q in range(M):
            direction[q, span] = remain[q, span] * inverse[q, 0:1, :] + beta * direction[q, span]
        return fresh

    def iterate(step, inners):
        slot = lax.rem(step, 2)
        results = []
        for stream, inner in zip(streams, inners):
            results.append(advance(stream, slot, inner))
            send(stream, 1 - slot, apply(stream))
        return tuple(results)

    inners = lax.fori_loop(1, ITERS, iterate, tuple(begin(stream) for stream in streams))
    span = pl.ds(blk * half, half)

    def away(stream, k):
        i, place, _ = stream
        source, target = solution.at[span, place], books.at[mine, span, place]
        return remote(source, target, far_send.at[i, k], far_recv.at[i, k], far(k))

    for stream, inner in zip(streams, inners):
        advance(stream, ITERS % 2, inner)
        for k in range(1, ncg):
            away(stream, k).start()

    for q in range(M):
        value = solution[q]
        books[mine, q] = value
        high = value.astype(BF16).astype(F32)
        team_parts[q] = jnp.concatenate([high, value - high], axis=0).astype(BF16)
    for k in range(1, ncg):
        team_copy(k).wait()
    size = min(256, share)
    short = lax.broadcasted_iota(jnp.int32, (K, size), 0).astype(F32).astype(BF16)

    def squares(turn, total):
        c, first = lax.div(turn, share // size), lax.rem(turn, share // size) * size
        source = (bases + c) * gsz + member
        at = pl.ds(pl.multiple_of(blk * share + first, size), size)
        value = jnp.zeros((2 * cols, size), F32)
        for q in range(M):
            row = codes_all[source, q : q + 1, at].astype(F32).astype(BF16)
            value = value + jnp.dot(team_parts[q], hot_t(row, short), preferred_element_type=F32)
        residual = crew[c, :, pl.ds(pl.multiple_of(first, size), size)] - (value[:cols] + value[cols:])
        return total + mass_all[source, :, at] * (residual * residual)

    total = lax.fori_loop(0, ncg * (share // size), squares, jnp.zeros((cols, size), F32))
    pairs[blk] = jnp.broadcast_to(jnp.sum(total, keepdims=True), (8, 128))
    beside = [
        remote(pairs.at[blk], pairs.at[blk], pair_send.at[db], pair_recv.at[db], {"blk": lax.rem(blk + db, nblk)})
        for db in range(1, nblk)
    ]
    for copy in beside:
        copy.start()
    for copy in beside:
        copy.wait()
    both = pairs[0]
    for b in range(1, nblk):
        both = both + pairs[b]
    gathered[me] = both

    def sum_copy(k):
        row = gathered.at[me, pl.ds(0, 1)]
        return remote(row, row, sum_send.at[k], sum_recv.at[k], chip(k))

    loop(lambda k: sum_copy(k).start())

    relays = []
    for stream in streams:
        i, place, _ = stream
        for k in range(1, ncg):
            away(stream, k).wait_recv()
            there = books.at[lax.rem(mine - k + ncg, ncg), span, place]
            for db in range(1, nblk):
                relay = remote(there, there, near_send.at[i, k, db], near_recv.at[i, k, db], team(0, db))
                relay.start()
                relays.append(relay)
    for relay in relays:
        relay.wait()

    for q in range(M):
        value = jnp.concatenate([books[c, q] for c in range(ncg)], axis=0)
        book_out[q] = value
        high, low = split2(value)
        parts[q, :width, :] = high
        parts[q, width:, :] = low

    def rebuild(turn):
        at = pl.ds(pl.multiple_of(turn * size, size), size)
        value = jnp.zeros((2 * width, size), F32)
        for q in range(M):
            row = codes_ref[q : q + 1, at].astype(F32).astype(BF16)
            value = value + jnp.dot(parts[q], hot_t(row, short), preferred_element_type=F32)
        residual_out[:, at] = vectors_ref[:, at] - (value[:width] + value[width:])

    pl.loop(0, rows // size)(rebuild)
    for stream in streams:
        for k in range(1, ncg):
            away(stream, k).wait_send()

    def drain(k):
        codes_copy(k).wait_send()
        mass_copy(k).wait_send()
        piece_copy(k).wait_send()
        for copy in passes(k):
            copy.wait_send()

    loop(drain)
    loop(lambda k: sum_copy(k).wait())
    final = lax.fori_loop(1, n, lambda s, value: value + gathered[s, 0:1], gathered[0, 0:1])
    sum_out[...] = jnp.broadcast_to(final / (whole * width), (8, 128))


def store(books_ref, residual_ref, sum_ref, books_out, residual_out, sum_out, sems):
    copies = [
        pltpu.make_async_copy(books_ref, books_out, sems.at[0]),
        pltpu.make_async_copy(residual_ref, residual_out, sems.at[1]),
    ]
    for copy in copies:
        copy.start()
    sum_out[...] = sum_ref[0:1, 0:1]
    for copy in copies:
        copy.wait()


def body(vectors, codes, weights, ridge):
    rows, width = vectors.shape
    n, nblk = lax.axis_size("dp"), lax.axis_size("blk")
    gsz = M // nblk
    ncg = column_groups(n // gsz, width)
    cols = width // ncg
    shape = jax.ShapeDtypeStruct
    dma = pltpu.SemaphoreType.DMA
    state = pltpu.VMEM((M, cols, K), F32)
    books, residual, distortion = pl.pallas_call(
        functools.partial(kernel, n, nblk, ncg),
        out_shape=(pltpu.VMEM((M, width, K), F32), pltpu.VMEM((width, rows), F32), pltpu.VMEM((8, 128), F32)),
        in_specs=[pl.BlockSpec(memory_space=pltpu.SMEM)] + [vmem()] * 3,
        out_specs=(vmem(),) * 3,
        scratch_shapes=[
            pltpu.VMEM((1, rows), F32),
            pltpu.VMEM((n, M, rows), jnp.int32),
            pltpu.VMEM((n, 1, rows), F32),
            pltpu.VMEM((ncg, gsz, cols, K), F32),
            pltpu.VMEM((n, cols, K), F32),
            pltpu.VMEM((M * K, K), F32),
            pltpu.VMEM((M * K, 2 * K), BF16),
            pltpu.VMEM((2, M, cols, K), F32),
            state,
            state,
            state,
            pltpu.VMEM((M, 8, K), F32),
            pltpu.VMEM((ncg, M, cols, K), F32),
            pltpu.VMEM((M, 2 * width, K), BF16),
            pltpu.VMEM((n, 8, 128), F32),
            dma((3, n)),
            dma((3, n)),
            dma((2, 3, M)),
            dma((2, 3, M)),
            dma((cols // 8, ncg)),
            dma((cols // 8, ncg)),
            dma((cols // 8, ncg, nblk)),
            dma((cols // 8, ncg, nblk)),
            dma((n,)),
            dma((n,)),
            dma((2, nblk, n)),
            dma((2, nblk, n)),
            pltpu.VMEM((8, K), F32),
            pltpu.VMEM((ncg, cols, rows // nblk), F32),
            pltpu.VMEM((M, 2 * cols, K), BF16),
            pltpu.VMEM((nblk, 8, 128), F32),
            dma((ncg,)),
            dma((ncg,)),
            dma((nblk,)),
            dma((nblk,)),
        ],
        compiler_params=pltpu.CompilerParams(collective_id=0, has_side_effects=True),
        name="update",
    )(ridge, codes.T, weights, vectors.T)
    books, residual, distortion = pl.pallas_call(
        store,
        out_shape=(shape((M, width, K), F32), shape((width, rows), F32), shape((1, 1), F32)),
        in_specs=[vmem()] * 3,
        out_specs=(pl.BlockSpec(memory_space=pl.ANY), pl.BlockSpec(memory_space=pl.ANY), vmem()),
        scratch_shapes=[dma((2,))],
        name="store",
    )(*(pltpu.with_memory_space_constraint(value, pltpu.VMEM) for value in (books, residual, distortion)))
    return (books.transpose(0, 2, 1), residual.T, distortion[0, 0])


def solution(mesh):
    return jax.shard_map(
        body,
        mesh=mesh,
        in_specs=(P("dp", None), P("dp", None), P("dp"), P()),
        out_specs=(P(), P("dp", None), P()),
        check_vma=False,
    )
```

```python
import functools

import jax
import jax.numpy as jnp
from jax import lax
from jax.experimental import pallas as pl
from jax.experimental.pallas import tpu as pltpu
from jax.sharding import PartitionSpec as P

K = 256
M = 8
ITERS = 8
LATE = 3
MESH = pl.DeviceIdType.MESH
HIGH = lax.Precision.HIGHEST
F32 = jnp.float32
BF16 = jnp.bfloat16
NT = (((1,), (1,)), ((), ()))


def vmem():
    return pl.BlockSpec(memory_space=pltpu.VMEM)


def split2(value):
    high = value.astype(BF16)
    low = (value - high.astype(F32)).astype(BF16)
    return high, low


def split3(value):
    high = value.astype(BF16)
    rest = value - high.astype(F32)
    middle = rest.astype(BF16)
    low = (rest - middle.astype(F32)).astype(BF16)
    return high, middle, low


def column_groups(groups, width):
    best = 1
    for count in range(1, groups + 1):
        if groups % count == 0 and width % count == 0 and (width // count) % 8 == 0:
            best = count
    return best


def hot_t(row, levels):
    return jnp.where(levels == row, jnp.ones((), BF16), jnp.zeros((), BF16))


def flip(value, mask, size):
    total, digit = 0, 1
    while digit < size:
        total = total + digit * lax.rem(value // digit + mask // digit, 2)
        digit *= 2
    return total


def column(pieces):
    total = pieces[0]
    for piece in pieces[1:]:
        total = total + piece
    return jnp.sum(total, axis=1, keepdims=True)


def kernel(n, nblk, ncg, ridge_ref, codes_in, weights_ref, vectors_in, book_out, residual_out, sum_out,
           codes_ref, vectors_ref, load_sem, mass_ref, codes_all, mass_all, part, pieces, gram, halves, swap, solution, remain, direction, inverse,
           books, parts, gathered, send_sem, recv_sem, swap_send, swap_recv, far_send, far_recv,
           near_send, near_recv, sum_send, sum_recv, pass_send, pass_recv, counts, crew, team_parts, pairs,
           team_send, team_recv, pair_send, pair_recv):
    width, rows = vectors_in.shape
    gsz = M // nblk
    cols = width // ncg
    me = lax.axis_index("dp")
    blk = lax.axis_index("blk")
    group, member = me // gsz, lax.rem(me, gsz)
    book = nblk * member + blk
    mine = lax.rem(group, ncg)
    bases = group - mine
    half = M // nblk
    peers = [(dm, db) for dm in range(gsz - 1, -1, -1) for db in range(nblk - 1, -1, -1) if (dm, db) != (0, 0)]

    def chip(k):
        return {"dp": flip(me, k, n)}

    def team(dm, db):
        return {"dp": group * gsz + flip(member, dm, gsz), "blk": lax.rem(blk + db, nblk)}

    def far(k):
        return {"dp": (bases + lax.rem(mine + k, ncg)) * gsz + member, "blk": blk}

    def remote(source, target, send, recv, to):
        return pltpu.make_async_remote_copy(
            src_ref=source, dst_ref=target, send_sem=send, recv_sem=recv, device_id=to, device_id_type=MESH
        )

    def loop(function):
        def step(k, carry):
            function(k)
            return carry

        lax.fori_loop(1, n, step, 0)

    barrier = pltpu.get_barrier_semaphore()
    mass_ref[...] = weights_ref[...].astype(F32).reshape(1, rows)
    loop(lambda k: pl.semaphore_signal(barrier, inc=1, device_id=chip(k), device_id_type=MESH))
    others = [(dm, db) for dm, db in peers if db]
    for dm, db in others:
        pl.semaphore_signal(barrier, inc=1, device_id=team(dm, db), device_id_type=MESH)

    loads = [
        pltpu.make_async_copy(codes_in, codes_ref, load_sem.at[0]),
        pltpu.make_async_copy(vectors_in, vectors_ref, load_sem.at[1]),
    ]
    for copy in loads:
        copy.start()
    for copy in loads:
        copy.wait()
    triple = jnp.concatenate(split3(vectors_ref[...]), axis=0)
    levels = lax.broadcasted_iota(jnp.int32, (K, rows), 0).astype(F32).astype(BF16)

    def spread(row, mass):
        return jnp.where(levels == row.astype(F32).astype(BF16), jnp.broadcast_to(mass, (K, rows)), jnp.zeros((), BF16))

    for m in range(gsz):
        hot = spread(codes_ref[pl.ds(nblk * m + blk, 1), :], mass_ref[...].astype(BF16))
        sums = lax.dot_general(triple, hot, NT, preferred_element_type=F32)
        total = sums[:width] + sums[width : 2 * width] + sums[2 * width :]
        for c in range(ncg):
            part[c, m] = total[c * cols : (c + 1) * cols]
    pl.semaphore_wait(barrier, n - 1 + len(others))

    share = rows // nblk
    lanes = pl.ds(pl.multiple_of(blk * share, share), share)

    def codes_copy(k):
        source, target = codes_ref.at[:, lanes], codes_all.at[me, :, lanes]
        return remote(source, target, send_sem.at[0, k], recv_sem.at[0, k], chip(k))

    def mass_copy(k):
        source, target = mass_ref.at[:, lanes], mass_all.at[me, :, lanes]
        return remote(source, target, send_sem.at[1, k], recv_sem.at[1, k], chip(k))

    def passes(k):
        there = chip(k)["dp"]
        copies = []
        for db in range(1, nblk):
            for i, array in enumerate((codes_all, mass_all)):
                piece = array.at[there, :, lanes]
                to = {"blk": lax.rem(blk + db, nblk)}
                copies.append(remote(piece, piece, pass_send.at[i, db, k], pass_recv.at[i, db, k], to))
        return copies

    def pass_on(k):
        codes_copy(k).wait_recv()
        mass_copy(k).wait_recv()
        for copy in passes(k):
            copy.start()

    def piece_copy(k):
        to = chip(k)["dp"]
        piece = part.at[lax.rem(to // gsz, ncg), lax.rem(to, gsz)]
        return remote(piece, pieces.at[me], send_sem.at[2, k], recv_sem.at[2, k], chip(k))

    def send_codes(k):
        codes_copy(k).start()
        mass_copy(k).start()

    loop(send_codes)
    loop(lambda k: piece_copy(k).start())

    codes_all[me] = codes_ref[...]
    mass_all[me] = mass_ref[...]
    pieces[me] = part[mine, member]
    gram[...] = jnp.zeros_like(gram)

    def block(q):
        return pl.ds(pl.multiple_of(q * K, K), K)

    def accumulate(source):
        weighted = spread(codes_all[source, pl.ds(book, 1), :], mass_all[source].astype(BF16))
        for j in range(1, M):
            other = lax.rem(book + j, M)
            hot = spread(codes_all[source, pl.ds(other, 1), :], jnp.ones((1, 1), BF16))
            gram[block(other), :] += lax.dot_general(hot, weighted, NT, preferred_element_type=F32)

    accumulate(me)
    pass_on(1)

    streams = [(i, pl.ds(first, last - first), last - first) for i, (first, last) in enumerate([(c, c + 8) for c in range(0, cols, 8)])]

    def copies(stream, slot):
        i, span, _ = stream
        here = swap.at[slot, book, span]
        return [
            remote(here, here, swap_send.at[slot, i, j], swap_recv.at[slot, i, j], team(dm, db))
            for j, (dm, db) in enumerate(peers)
        ]

    def send(stream, slot, value):
        swap[slot, book, stream[1]] = value
        for copy in copies(stream, slot):
            copy.start()

    def open_streams():
        loop(lambda k: piece_copy(k).wait_recv())
        right = lax.fori_loop(1, n, lambda s, total: total + pieces[s], pieces[0])
        for stream in streams:
            first = stream[1].start
            send(stream, 0, right[first : first + stream[2]])

    def arrive(k):
        pl.when(k == max(n - LATE, 1))(open_streams)
        for copy in passes(k):
            copy.wait_recv()

        @pl.when(k + 1 < n)
        def _():
            pass_on(k + 1)

        accumulate(chip(k)["dp"])

    loop(arrive)

    own = jnp.sum(gram[block(lax.rem(book + 1, M)), :], axis=0, keepdims=True)
    inverse[book] = jnp.broadcast_to(own, (8, K))
    counts[...] = inverse[book]
    ones = jnp.ones((8, K), BF16)
    for j in range(1, M):
        other = lax.rem(book + j, M)
        high, low, rest = split3(gram[block(other), :])
        halves[(j - 1) * K : j * K, :K] = high
        halves[(j - 1) * K : j * K, K:] = low
        total = None
        for piece in (high, low, rest):
            term = lax.dot_general(ones, piece, NT, preferred_element_type=F32)
            total = term if total is None else total + term
        inverse[other] = total
    whole = jnp.sum(inverse[0, 0:1, :])
    lam = ridge_ref[0] * (whole / K)
    for q in range(M):
        inverse[q] = 1.0 / (inverse[q] + lam)

    def band(c):
        return pl.ds(pl.multiple_of(c * cols, 8), cols)

    def team_copy(k):
        source, target = vectors_ref.at[band(lax.rem(mine + k, ncg)), lanes], crew.at[mine]
        return remote(source, target, team_send.at[k], team_recv.at[k], far(k))

    for k in range(1, ncg):
        team_copy(k).start()
    crew[mine] = vectors_ref[band(mine), lanes]

    def receive(stream, slot):
        for copy in copies(stream, slot):
            copy.wait()

    def apply(stream):
        _, span, size = stream
        lefts = []
        for j in range(1, M):
            lefts.append(jnp.concatenate(split2(direction[lax.rem(book + j, M), span]), axis=0))
        product = jnp.dot(jnp.concatenate(lefts, axis=1), halves[...], preferred_element_type=F32)
        total = (product[:size, :K] + product[size:, :K]) + (product[:size, K:] + product[size:, K:])
        return total + counts[0:1, :] * direction[book, span]

    def begin(stream):
        _, span, _ = stream
        receive(stream, 0)
        terms = []
        for q in range(M):
            r = swap[0, q, span]
            z = r * inverse[q, 0:1, :]
            remain[q, span] = r
            direction[q, span] = z
            solution[q, span] = jnp.zeros_like(r)
            terms.append(r * z)
        send(stream, 1, apply(stream))
        return column(terms)

    def advance(stream, slot, inner):
        _, span, _ = stream
        receive(stream, slot)
        terms = []
        for q in range(M):
            d = direction[q, span]
            terms.append(d * (swap[slot, q, span] + lam * d))
        alpha = inner / column(terms)
        terms = []
        for q in range(M):
            d = direction[q, span]
            r = remain[q, span] - alpha * (swap[slot, q, span] + lam * d)
            solution[q, span] = solution[q, span] + alpha * d
            remain[q, span] = r
            terms.append(r * (r * inverse[q, 0:1, :]))
        fresh = column(terms)
        beta = fresh / inner
        for q in range(M):
            direction[q, span] = remain[q, span] * inverse[q, 0:1, :] + beta * direction[q, span]
        return fresh

    def finish(stream, slot, inner):
        _, span, _ = stream
        receive(stream, slot)
        terms = []
        for q in range(M):
            d = direction[q, span]
            terms.append(d * (swap[slot, q, span] + lam * d))
        alpha = inner / column(terms)
        for q in range(M):
            books[mine, q, span] = solution[q, span] + alpha * direction[q, span]

    def iterate(step, inners):
        slot = lax.rem(step, 2)
        results = []
        for stream, inner in zip(streams, inners):
            results.append(advance(stream, slot, inner))
            send(stream, 1 - slot, apply(stream))
        return tuple(results)

    inners = lax.fori_loop(1, ITERS, iterate, tuple(begin(stream) for stream in streams))
    span = pl.ds(blk * half, half)

    def away(stream, k):
        i, place, _ = stream
        piece = books.at[mine, span, place]
        return remote(piece, piece, far_send.at[i, k], far_recv.at[i, k], far(k))

    for stream, inner in zip(streams, inners):
        finish(stream, ITERS % 2, inner)
        for k in range(1, ncg):
            away(stream, k).start()

    for q in range(M):
        value = books[mine, q]
        high = value.astype(BF16).astype(F32)
        team_parts[q] = jnp.concatenate([high, value - high], axis=0).astype(BF16)
    for k in range(1, ncg):
        team_copy(k).wait()
    size = min(256, share)
    short = lax.broadcasted_iota(jnp.int32, (K, size), 0).astype(F32).astype(BF16)

    def squares(turn, total):
        c, first = lax.div(turn, share // size), lax.rem(turn, share // size) * size
        source = (bases + c) * gsz + member
        at = pl.ds(pl.multiple_of(blk * share + first, size), size)
        value = jnp.zeros((2 * cols, size), F32)
        for q in range(M):
            row = codes_all[source, q : q + 1, at].astype(F32).astype(BF16)
            value = value + jnp.dot(team_parts[q], hot_t(row, short), preferred_element_type=F32)
        residual = crew[c, :, pl.ds(pl.multiple_of(first, size), size)] - (value[:cols] + value[cols:])
        return total + mass_all[source, :, at] * (residual * residual)

    total = lax.fori_loop(0, ncg * (share // size), squares, jnp.zeros((cols, size), F32))
    pairs[blk] = jnp.broadcast_to(jnp.sum(total, keepdims=True), (8, 128))
    beside = [
        remote(pairs.at[blk], pairs.at[blk], pair_send.at[db], pair_recv.at[db], {"blk": lax.rem(blk + db, nblk)})
        for db in range(1, nblk)
    ]
    for copy in beside:
        copy.start()
    for copy in beside:
        copy.wait()
    both = pairs[0]
    for b in range(1, nblk):
        both = both + pairs[b]
    gathered[me] = both

    def sum_copy(k):
        row = gathered.at[me, pl.ds(0, 1)]
        return remote(row, row, sum_send.at[k], sum_recv.at[k], chip(k))

    loop(lambda k: sum_copy(k).start())

    relays = []
    for stream in streams:
        i, place, _ = stream
        for k in range(1, ncg):
            away(stream, k).wait_recv()
            there = books.at[lax.rem(mine - k + ncg, ncg), span, place]
            for db in range(1, nblk):
                relay = remote(there, there, near_send.at[i, k, db], near_recv.at[i, k, db], team(0, db))
                relay.start()
                relays.append(relay)
    for relay in relays:
        relay.wait()

    for q in range(M):
        value = jnp.concatenate([books[c, q] for c in range(ncg)], axis=0)
        book_out[q] = value
        high, low = split2(value)
        parts[q, :width, :] = high
        parts[q, width:, :] = low

    def rebuild(turn):
        at = pl.ds(pl.multiple_of(turn * size, size), size)
        value = jnp.zeros((2 * width, size), F32)
        for q in range(M):
            row = codes_ref[q : q + 1, at].astype(F32).astype(BF16)
            value = value + jnp.dot(parts[q], hot_t(row, short), preferred_element_type=F32)
        residual_out[:, at] = vectors_ref[:, at] - (value[:width] + value[width:])

    pl.loop(0, rows // size)(rebuild)
    for stream in streams:
        for k in range(1, ncg):
            away(stream, k).wait_send()

    def drain(k):
        codes_copy(k).wait_send()
        mass_copy(k).wait_send()
        piece_copy(k).wait_send()
        for copy in passes(k):
            copy.wait_send()

    loop(drain)
    loop(lambda k: sum_copy(k).wait())
    final = lax.fori_loop(1, n, lambda s, value: value + gathered[s, 0:1], gathered[0, 0:1])
    sum_out[...] = jnp.broadcast_to(final / (whole * width), (8, 128))


def store(books_ref, residual_ref, sum_ref, books_out, residual_out, sum_out, sems):
    copies = [
        pltpu.make_async_copy(books_ref, books_out, sems.at[0]),
        pltpu.make_async_copy(residual_ref, residual_out, sems.at[1]),
    ]
    for copy in copies:
        copy.start()
    sum_out[...] = sum_ref[0:1, 0:1]
    for copy in copies:
        copy.wait()


def body(vectors, codes, weights, ridge):
    rows, width = vectors.shape
    n, nblk = lax.axis_size("dp"), lax.axis_size("blk")
    gsz = M // nblk
    ncg = column_groups(n // gsz, width)
    cols = width // ncg
    shape = jax.ShapeDtypeStruct
    dma = pltpu.SemaphoreType.DMA
    state = pltpu.VMEM((M, cols, K), F32)
    books, residual, distortion = pl.pallas_call(
        functools.partial(kernel, n, nblk, ncg),
        out_shape=(pltpu.VMEM((M, width, K), F32), pltpu.VMEM((width, rows), F32), pltpu.VMEM((8, 128), F32)),
        in_specs=[pl.BlockSpec(memory_space=pltpu.SMEM), pl.BlockSpec(memory_space=pl.ANY), vmem(), pl.BlockSpec(memory_space=pl.ANY)],
        out_specs=(vmem(),) * 3,
        scratch_shapes=[
            pltpu.VMEM((M, rows), jnp.int32),
            pltpu.VMEM((width, rows), F32),
            dma((2,)),
            pltpu.VMEM((1, rows), F32),
            pltpu.VMEM((n, M, rows), jnp.int32),
            pltpu.VMEM((n, 1, rows), F32),
            pltpu.VMEM((ncg, gsz, cols, K), F32),
            pltpu.VMEM((n, cols, K), F32),
            pltpu.VMEM((M * K, K), F32),
            pltpu.VMEM(((M - 1) * K, 2 * K), BF16),
            pltpu.VMEM((2, M, cols, K), F32),
            state,
            state,
            state,
            pltpu.VMEM((M, 8, K), F32),
            pltpu.VMEM((ncg, M, cols, K), F32),
            pltpu.VMEM((M, 2 * width, K), BF16),
            pltpu.VMEM((n, 8, 128), F32),
            dma((3, n)),
            dma((3, n)),
            dma((2, 3, M)),
            dma((2, 3, M)),
            dma((cols // 8, ncg)),
            dma((cols // 8, ncg)),
            dma((cols // 8, ncg, nblk)),
            dma((cols // 8, ncg, nblk)),
            dma((n,)),
            dma((n,)),
            dma((2, nblk, n)),
            dma((2, nblk, n)),
            pltpu.VMEM((8, K), F32),
            pltpu.VMEM((ncg, cols, rows // nblk), F32),
            pltpu.VMEM((M, 2 * cols, K), BF16),
            pltpu.VMEM((nblk, 8, 128), F32),
            dma((ncg,)),
            dma((ncg,)),
            dma((nblk,)),
            dma((nblk,)),
        ],
        compiler_params=pltpu.CompilerParams(collective_id=0, has_side_effects=True),
        name="update",
    )(ridge, codes.T, weights, vectors.T)
    books, residual, distortion = pl.pallas_call(
        store,
        out_shape=(shape((M, width, K), F32), shape((width, rows), F32), shape((1, 1), F32)),
        in_specs=[vmem()] * 3,
        out_specs=(pl.BlockSpec(memory_space=pl.ANY), pl.BlockSpec(memory_space=pl.ANY), vmem()),
        scratch_shapes=[dma((2,))],
        name="store",
    )(*(pltpu.with_memory_space_constraint(value, pltpu.VMEM) for value in (books, residual, distortion)))
    return (books.transpose(0, 2, 1), residual.T, distortion[0, 0])


def solution(mesh):
    return jax.shard_map(
        body,
        mesh=mesh,
        in_specs=(P("dp", None), P("dp", None), P("dp"), P()),
        out_specs=(P(), P("dp", None), P()),
        check_vma=False,
    )
```

```python
import functools

import jax
import jax.numpy as jnp
from jax import lax
from jax.experimental import pallas as pl
from jax.experimental.pallas import tpu as pltpu
from jax.sharding import PartitionSpec as P

K = 256
M = 8
ITERS = 8
LATE = 3
MESH = pl.DeviceIdType.MESH
HIGH = lax.Precision.HIGHEST
F32 = jnp.float32
BF16 = jnp.bfloat16
NT = (((1,), (1,)), ((), ()))


def vmem():
    return pl.BlockSpec(memory_space=pltpu.VMEM)


def split2(value):
    high = value.astype(BF16)
    low = (value - high.astype(F32)).astype(BF16)
    return high, low


def split3(value):
    high = value.astype(BF16)
    rest = value - high.astype(F32)
    middle = rest.astype(BF16)
    low = (rest - middle.astype(F32)).astype(BF16)
    return high, middle, low


def column_groups(groups, width):
    best = 1
    for count in range(1, groups + 1):
        if groups % count == 0 and width % count == 0 and (width // count) % 8 == 0:
            best = count
    return best


def hot_t(row, levels):
    return jnp.where(levels == row, jnp.ones((), BF16), jnp.zeros((), BF16))


def flip(value, mask, size):
    total, digit = 0, 1
    while digit < size:
        total = total + digit * lax.rem(value // digit + mask // digit, 2)
        digit *= 2
    return total


def column(pieces):
    total = pieces[0]
    for piece in pieces[1:]:
        total = total + piece
    return jnp.sum(total, axis=1, keepdims=True)


def kernel(n, nblk, ncg, ridge_ref, codes_in, weights_ref, vectors_in, book_out, residual_out, sum_out,
           codes_ref, vectors_ref, load_sem, mass_ref, codes_all, mass_all, part, pieces, gram, halves, swap, solution, remain, direction, inverse,
           books, parts, gathered, send_sem, recv_sem, swap_send, swap_recv, far_send, far_recv,
           near_send, near_recv, sum_send, sum_recv, pass_send, pass_recv, counts, crew, team_parts, pairs,
           team_send, team_recv, pair_send, pair_recv):
    width, rows = vectors_in.shape
    gsz = M // nblk
    cols = width // ncg
    me = lax.axis_index("dp")
    blk = lax.axis_index("blk")
    group, member = me // gsz, lax.rem(me, gsz)
    book = nblk * member + blk
    mine = lax.rem(group, ncg)
    bases = group - mine
    half = M // nblk
    peers = [(dm, db) for dm in range(gsz - 1, -1, -1) for db in range(nblk - 1, -1, -1) if (dm, db) != (0, 0)]

    def chip(k):
        return {"dp": flip(me, k, n)}

    def team(dm, db):
        return {"dp": group * gsz + flip(member, dm, gsz), "blk": lax.rem(blk + db, nblk)}

    def far(k):
        return {"dp": (bases + lax.rem(mine + k, ncg)) * gsz + member, "blk": blk}

    def remote(source, target, send, recv, to):
        return pltpu.make_async_remote_copy(
            src_ref=source, dst_ref=target, send_sem=send, recv_sem=recv, device_id=to, device_id_type=MESH
        )

    def loop(function):
        def step(k, carry):
            function(k)
            return carry

        lax.fori_loop(1, n, step, 0)

    barrier = pltpu.get_barrier_semaphore()
    mass_ref[...] = weights_ref[...].astype(F32).reshape(1, rows)
    loop(lambda k: pl.semaphore_signal(barrier, inc=1, device_id=chip(k), device_id_type=MESH))
    others = [(dm, db) for dm, db in peers if db]
    for dm, db in others:
        pl.semaphore_signal(barrier, inc=1, device_id=team(dm, db), device_id_type=MESH)

    loads = [
        pltpu.make_async_copy(codes_in, codes_ref, load_sem.at[0]),
        pltpu.make_async_copy(vectors_in, vectors_ref, load_sem.at[1]),
    ]
    for copy in loads:
        copy.start()
    for copy in loads:
        copy.wait()
    triple = jnp.concatenate(split3(vectors_ref[...]), axis=0)
    levels = lax.broadcasted_iota(jnp.int32, (K, rows), 0).astype(F32).astype(BF16)

    def spread(row, mass):
        return jnp.where(levels == row.astype(F32).astype(BF16), jnp.broadcast_to(mass, (K, rows)), jnp.zeros((), BF16))

    for m in range(gsz):
        hot = spread(codes_ref[pl.ds(nblk * m + blk, 1), :], mass_ref[...].astype(BF16))
        sums = lax.dot_general(triple, hot, NT, preferred_element_type=F32)
        total = sums[:width] + sums[width : 2 * width] + sums[2 * width :]
        for c in range(ncg):
            part[c, m] = total[c * cols : (c + 1) * cols]
    pl.semaphore_wait(barrier, n - 1 + len(others))

    share = rows // nblk
    lanes = pl.ds(pl.multiple_of(blk * share, share), share)

    def codes_copy(k):
        source, target = codes_ref.at[:, lanes], codes_all.at[me, :, lanes]
        return remote(source, target, send_sem.at[0, k], recv_sem.at[0, k], chip(k))

    def mass_copy(k):
        source, target = mass_ref.at[:, lanes], mass_all.at[me, :, lanes]
        return remote(source, target, send_sem.at[1, k], recv_sem.at[1, k], chip(k))

    def passes(k):
        there = chip(k)["dp"]
        copies = []
        for db in range(1, nblk):
            for i, array in enumerate((codes_all, mass_all)):
                piece = array.at[there, :, lanes]
                to = {"blk": lax.rem(blk + db, nblk)}
                copies.append(remote(piece, piece, pass_send.at[i, db, k], pass_recv.at[i, db, k], to))
        return copies

    def pass_on(k):
        codes_copy(k).wait_recv()
        mass_copy(k).wait_recv()
        for copy in passes(k):
            copy.start()

    def piece_copy(k):
        to = chip(k)["dp"]
        piece = part.at[lax.rem(to // gsz, ncg), lax.rem(to, gsz)]
        return remote(piece, pieces.at[me], send_sem.at[2, k], recv_sem.at[2, k], chip(k))

    def send_codes(k):
        codes_copy(k).start()
        mass_copy(k).start()

    loop(send_codes)
    loop(lambda k: piece_copy(k).start())

    codes_all[me] = codes_ref[...]
    mass_all[me] = mass_ref[...]
    pieces[me] = part[mine, member]
    gram[...] = jnp.zeros_like(gram)

    def block(q):
        return pl.ds(pl.multiple_of(q * K, K), K)

    def accumulate(source):
        weighted = spread(codes_all[source, pl.ds(book, 1), :], mass_all[source].astype(BF16))
        for j in range(1, M):
            other = lax.rem(book + j, M)
            hot = spread(codes_all[source, pl.ds(other, 1), :], jnp.ones((1, 1), BF16))
            gram[block(other), :] += lax.dot_general(hot, weighted, NT, preferred_element_type=F32)

    accumulate(me)
    pass_on(1)

    streams = [(i, pl.ds(first, last - first), last - first) for i, (first, last) in enumerate([(c, c + 8) for c in range(0, cols, 8)])]

    def copies(stream, slot, short_form=False):
        i, span, _ = stream
        here = swap.at[slot, book, span] if not short_form else swap.at[slot, book, span, pl.ds(0, K // 2)]
        return [
            remote(here, here, swap_send.at[slot, i, j], swap_recv.at[slot, i, j], team(dm, db))
            for j, (dm, db) in enumerate(peers)
        ]

    def send(stream, slot, value, short_form=False):
        swap[slot, book, stream[1], : value.shape[1]] = value
        for copy in copies(stream, slot, short_form):
            copy.start()

    def open_streams():
        loop(lambda k: piece_copy(k).wait_recv())
        right = lax.fori_loop(1, n, lambda s, total: total + pieces[s], pieces[0])
        for stream in streams:
            first = stream[1].start
            send(stream, 0, right[first : first + stream[2]])

    def arrive(k):
        pl.when(k == max(n - LATE, 1))(open_streams)
        for copy in passes(k):
            copy.wait_recv()

        @pl.when(k + 1 < n)
        def _():
            pass_on(k + 1)

        accumulate(chip(k)["dp"])

    loop(arrive)

    own = jnp.sum(gram[block(lax.rem(book + 1, M)), :], axis=0, keepdims=True)
    inverse[book] = jnp.broadcast_to(own, (8, K))
    counts[...] = inverse[book]
    ones = jnp.ones((8, K), BF16)
    for j in range(1, M):
        other = lax.rem(book + j, M)
        high, low, rest = split3(gram[block(other), :])
        halves[(j - 1) * K : j * K, :K] = high
        halves[(j - 1) * K : j * K, K:] = low
        total = None
        for piece in (high, low, rest):
            term = lax.dot_general(ones, piece, NT, preferred_element_type=F32)
            total = term if total is None else total + term
        inverse[other] = total
    whole = jnp.sum(inverse[0, 0:1, :])
    lam = ridge_ref[0] * (whole / K)
    for q in range(M):
        inverse[q] = 1.0 / (inverse[q] + lam)

    def band(c):
        return pl.ds(pl.multiple_of(c * cols, 8), cols)

    def team_copy(k):
        source, target = vectors_ref.at[band(lax.rem(mine + k, ncg)), lanes], crew.at[mine]
        return remote(source, target, team_send.at[k], team_recv.at[k], far(k))

    for k in range(1, ncg):
        team_copy(k).start()
    crew[mine] = vectors_ref[band(mine), lanes]

    def receive(stream, slot, short_form=False):
        for copy in copies(stream, slot, short_form):
            copy.wait()

    def apply(stream):
        _, span, size = stream
        lefts = []
        for j in range(1, M):
            lefts.append(jnp.concatenate(split2(direction[lax.rem(book + j, M), span]), axis=0))
        product = jnp.dot(jnp.concatenate(lefts, axis=1), halves[...], preferred_element_type=F32)
        total = (product[:size, :K] + product[size:, :K]) + (product[:size, K:] + product[size:, K:])
        return total + counts[0:1, :] * direction[book, span]

    def begin(stream):
        _, span, _ = stream
        receive(stream, 0)
        terms = []
        for q in range(M):
            r = swap[0, q, span]
            z = r * inverse[q, 0:1, :]
            remain[q, span] = r
            direction[q, span] = z
            solution[q, span] = jnp.zeros_like(r)
            terms.append(r * z)
        send(stream, 1, apply(stream))
        return column(terms)

    def advance(stream, slot, inner):
        _, span, _ = stream
        receive(stream, slot)
        terms = []
        for q in range(M):
            d = direction[q, span]
            terms.append(d * (swap[slot, q, span] + lam * d))
        alpha = inner / column(terms)
        terms = []
        for q in range(M):
            d = direction[q, span]
            r = remain[q, span] - alpha * (swap[slot, q, span] + lam * d)
            solution[q, span] = solution[q, span] + alpha * d
            remain[q, span] = r
            terms.append(r * (r * inverse[q, 0:1, :]))
        fresh = column(terms)
        beta = fresh / inner
        for q in range(M):
            direction[q, span] = remain[q, span] * inverse[q, 0:1, :] + beta * direction[q, span]
        return fresh

    def finish(stream, slot, inner):
        _, span, _ = stream
        receive(stream, slot, True)
        alpha = inner / column([swap[slot, q, span, : K // 2] for q in range(M)])
        for q in range(M):
            books[mine, q, span] = solution[q, span] + alpha * direction[q, span]

    def iterate(step, inners):
        slot = lax.rem(step, 2)
        results = []
        for stream, inner in zip(streams, inners):
            results.append(advance(stream, slot, inner))
            send(stream, 1 - slot, apply(stream))
        return tuple(results)

    def last(step, inners):
        slot = step % 2
        results = []
        for stream, inner in zip(streams, inners):
            results.append(advance(stream, slot, inner))
            d = direction[book, stream[1]]
            part = d * (apply(stream) + lam * d)
            send(stream, 1 - slot, part[:, : K // 2] + part[:, K // 2 :], True)
        return tuple(results)

    inners = lax.fori_loop(1, ITERS - 1, iterate, tuple(begin(stream) for stream in streams))
    inners = last(ITERS - 1, inners)
    span = pl.ds(blk * half, half)

    def away(stream, k):
        i, place, _ = stream
        piece = books.at[mine, span, place]
        return remote(piece, piece, far_send.at[i, k], far_recv.at[i, k], far(k))

    for stream, inner in zip(streams, inners):
        finish(stream, ITERS % 2, inner)
        for k in range(1, ncg):
            away(stream, k).start()

    for q in range(M):
        value = books[mine, q]
        high = value.astype(BF16).astype(F32)
        team_parts[q] = jnp.concatenate([high, value - high], axis=0).astype(BF16)
    for k in range(1, ncg):
        team_copy(k).wait()
    size = min(256, share)
    short = lax.broadcasted_iota(jnp.int32, (K, size), 0).astype(F32).astype(BF16)

    def squares(turn, total):
        c, first = lax.div(turn, share // size), lax.rem(turn, share // size) * size
        source = (bases + c) * gsz + member
        at = pl.ds(pl.multiple_of(blk * share + first, size), size)
        value = jnp.zeros((2 * cols, size), F32)
        for q in range(M):
            row = codes_all[source, q : q + 1, at].astype(F32).astype(BF16)
            value = value + jnp.dot(team_parts[q], hot_t(row, short), preferred_element_type=F32)
        residual = crew[c, :, pl.ds(pl.multiple_of(first, size), size)] - (value[:cols] + value[cols:])
        return total + mass_all[source, :, at] * (residual * residual)

    total = lax.fori_loop(0, ncg * (share // size), squares, jnp.zeros((cols, size), F32))
    pairs[blk] = jnp.broadcast_to(jnp.sum(total, keepdims=True), (8, 128))
    beside = [
        remote(pairs.at[blk], pairs.at[blk], pair_send.at[db], pair_recv.at[db], {"blk": lax.rem(blk + db, nblk)})
        for db in range(1, nblk)
    ]
    for copy in beside:
        copy.start()
    for copy in beside:
        copy.wait()
    both = pairs[0]
    for b in range(1, nblk):
        both = both + pairs[b]
    gathered[me] = both

    def sum_copy(k):
        row = gathered.at[me, pl.ds(0, 1)]
        return remote(row, row, sum_send.at[k], sum_recv.at[k], chip(k))

    loop(lambda k: sum_copy(k).start())

    relays = []
    for stream in streams:
        i, place, _ = stream
        for k in range(1, ncg):
            away(stream, k).wait_recv()
            there = books.at[lax.rem(mine - k + ncg, ncg), span, place]
            for db in range(1, nblk):
                relay = remote(there, there, near_send.at[i, k, db], near_recv.at[i, k, db], team(0, db))
                relay.start()
                relays.append(relay)
    for relay in relays:
        relay.wait()

    for q in range(M):
        value = jnp.concatenate([books[c, q] for c in range(ncg)], axis=0)
        book_out[q] = value
        high, low = split2(value)
        parts[:width, q * K : (q + 1) * K] = high
        parts[width:, q * K : (q + 1) * K] = low

    def rebuild(turn):
        at = pl.ds(pl.multiple_of(turn * size, size), size)
        hots = [hot_t(codes_ref[q : q + 1, at].astype(F32).astype(BF16), short) for q in range(M)]
        value = jnp.dot(parts[...], jnp.concatenate(hots, axis=0), preferred_element_type=F32)
        residual_out[:, at] = vectors_ref[:, at] - (value[:width] + value[width:])

    pl.loop(0, rows // size)(rebuild)
    for stream in streams:
        for k in range(1, ncg):
            away(stream, k).wait_send()

    def drain(k):
        codes_copy(k).wait_send()
        mass_copy(k).wait_send()
        piece_copy(k).wait_send()
        for copy in passes(k):
            copy.wait_send()

    loop(drain)
    loop(lambda k: sum_copy(k).wait())
    final = lax.fori_loop(1, n, lambda s, value: value + gathered[s, 0:1], gathered[0, 0:1])
    sum_out[...] = jnp.broadcast_to(final / (whole * width), (8, 128))


def store(books_ref, residual_ref, sum_ref, books_out, residual_out, sum_out, sems):
    copies = [
        pltpu.make_async_copy(books_ref, books_out, sems.at[0]),
        pltpu.make_async_copy(residual_ref, residual_out, sems.at[1]),
    ]
    for copy in copies:
        copy.start()
    sum_out[...] = sum_ref[0:1, 0:1]
    for copy in copies:
        copy.wait()


def body(vectors, codes, weights, ridge):
    rows, width = vectors.shape
    n, nblk = lax.axis_size("dp"), lax.axis_size("blk")
    gsz = M // nblk
    ncg = column_groups(n // gsz, width)
    cols = width // ncg
    shape = jax.ShapeDtypeStruct
    dma = pltpu.SemaphoreType.DMA
    state = pltpu.VMEM((M, cols, K), F32)
    books, residual, distortion = pl.pallas_call(
        functools.partial(kernel, n, nblk, ncg),
        out_shape=(pltpu.VMEM((M, width, K), F32), pltpu.VMEM((width, rows), F32), pltpu.VMEM((8, 128), F32)),
        in_specs=[pl.BlockSpec(memory_space=pltpu.SMEM), pl.BlockSpec(memory_space=pl.ANY), vmem(), pl.BlockSpec(memory_space=pl.ANY)],
        out_specs=(vmem(),) * 3,
        scratch_shapes=[
            pltpu.VMEM((M, rows), jnp.int32),
            pltpu.VMEM((width, rows), F32),
            dma((2,)),
            pltpu.VMEM((1, rows), F32),
            pltpu.VMEM((n, M, rows), jnp.int32),
            pltpu.VMEM((n, 1, rows), F32),
            pltpu.VMEM((ncg, gsz, cols, K), F32),
            pltpu.VMEM((n, cols, K), F32),
            pltpu.VMEM((M * K, K), F32),
            pltpu.VMEM(((M - 1) * K, 2 * K), BF16),
            pltpu.VMEM((2, M, cols, K), F32),
            state,
            state,
            state,
            pltpu.VMEM((M, 8, K), F32),
            pltpu.VMEM((ncg, M, cols, K), F32),
            pltpu.VMEM((2 * width, M * K), BF16),
            pltpu.VMEM((n, 8, 128), F32),
            dma((3, n)),
            dma((3, n)),
            dma((2, 3, M)),
            dma((2, 3, M)),
            dma((cols // 8, ncg)),
            dma((cols // 8, ncg)),
            dma((cols // 8, ncg, nblk)),
            dma((cols // 8, ncg, nblk)),
            dma((n,)),
            dma((n,)),
            dma((2, nblk, n)),
            dma((2, nblk, n)),
            pltpu.VMEM((8, K), F32),
            pltpu.VMEM((ncg, cols, rows // nblk), F32),
            pltpu.VMEM((M, 2 * cols, K), BF16),
            pltpu.VMEM((nblk, 8, 128), F32),
            dma((ncg,)),
            dma((ncg,)),
            dma((nblk,)),
            dma((nblk,)),
        ],
        compiler_params=pltpu.CompilerParams(collective_id=0, has_side_effects=True),
        name="update",
    )(ridge, codes.T, weights, vectors.T)
    books, residual, distortion = pl.pallas_call(
        store,
        out_shape=(shape((M, width, K), F32), shape((width, rows), F32), shape((1, 1), F32)),
        in_specs=[vmem()] * 3,
        out_specs=(pl.BlockSpec(memory_space=pl.ANY), pl.BlockSpec(memory_space=pl.ANY), vmem()),
        scratch_shapes=[dma((2,))],
        name="store",
    )(*(pltpu.with_memory_space_constraint(value, pltpu.VMEM) for value in (books, residual, distortion)))
    return (books.transpose(0, 2, 1), residual.T, distortion[0, 0])


def solution(mesh):
    return jax.shard_map(
        body,
        mesh=mesh,
        in_specs=(P("dp", None), P("dp", None), P("dp"), P()),
        out_specs=(P(), P("dp", None), P()),
        check_vma=False,
    )
```
